512 devices in a mesh: src: 64 (over z_hi, y, x, core), fac: 8 (over z_lo).
Axes of the slice: x: 4, y: 4, z: 16 (z_hi: 2, z_lo: 8; z = z_hi * 8 + z_lo), core: 2. Of those that a mesh axis runs over, the one named last changes fastest.
Arguments:
- lower_inverse: bfloat16 [8, 1024, 2, 1024], P('fac', 'src'), as said below
- coupling: bfloat16 [8, 1024, 2, 1024], P('fac', 'src'), as said below
- source_cell: int32 [8192], P('src'), may hold values from 0 to 8191
- source_wave: float32 [8192, 2], P('src'), may hold values from -6 to 6
- inflow_field: bfloat16 [8192, 2, 1024], P('src'), may hold values from -6 to 6
- receiver_cell: int32 [8192, 128], P('src'), may hold values from 0 to 8191
- observed: float32 [8192, 2, 128], P('src'), may hold values from -6 to 6
- adjoint: bfloat16 [8192, 8, 2, 1024], P('src', 'fac'), may hold values from -16 to 16
Outputs:
- wavefield: float32 [8192, 8, 2, 1024], P('src', 'fac')
- data_residual: float32 [8192, 2, 128], P('src')
- gradient: float32 [8, 1024], P('fac', 'src')
The draws below stay inside these ranges and needn't reach their ends.
Inputs may be any that keep to these rules, and one draw needn't show every extreme that they name: lower_inverse[i, j, p, k] is zero where k > j. coupling[i, j, p, k] is zero where k < j.
All inputs are finite; a program needn't handle non-finite values.
Results may differ from the reference program's by a relative error of at most 0.025.
Values may be sent and summed in bfloat16 or wider, within the bound.
No kernel may reach another device: no remote copies, remote signals or barrier semaphores. Data moves between devices by JAX's collectives and lax.ppermute only.
A program may use at most 64 MiB of HBM per device.

```python
import math
import jax
import jax.numpy as jnp
from jax import lax

BW = 1024
NREC = 128
NB = 8
NS = 8192


def draw_lower_inverse(key, part):
    first, second, third = jax.random.split(jax.random.fold_in(key, 11), 3)
    row_ids = jnp.arange(BW)[:, None]
    col_ids = jnp.arange(BW)[None, :]
    offdiag = jax.random.normal(first, (NB, 2, BW, BW), jnp.float32)
    real_diag = jax.random.uniform(second, (NB, BW), jnp.float32, 0.8, 1.25)
    imag_diag = jax.random.uniform(third, (NB, BW), jnp.float32, -0.3, 0.3)
    offdiag = offdiag * (0.5 / math.sqrt(BW))
    diagonal = jnp.stack([real_diag, imag_diag], axis=1)
    result = jnp.where(row_ids > col_ids, offdiag, 0.0) + jnp.where(row_ids == col_ids, diagonal[:, :, :, None], 0.0)
    return jnp.transpose(result, (0, 2, 1, 3)).astype(jnp.bfloat16)


def draw_coupling(key, part):
    first = jax.random.fold_in(key, 23)
    row_ids = jnp.arange(BW)[:, None]
    col_ids = jnp.arange(BW)[None, :]
    entries = jax.random.normal(first, (NB, 2, BW, BW), jnp.float32)
    entries = entries * (1.0 / math.sqrt(BW))
    result = jnp.where(row_ids <= col_ids, entries, 0.0)
    return jnp.transpose(result, (0, 2, 1, 3)).astype(jnp.bfloat16)


def place_ends(values, stream_key, low, largest):
    place = [jax.random.randint(jax.random.fold_in(stream_key, axis), (), 0, length) for axis, length in enumerate(values.shape)]
    main_axis = values.shape.index(max(values.shape))
    beside = place[:main_axis] + [(place[main_axis] + 1) % values.shape[main_axis]] + place[main_axis + 1:]
    return values.at[tuple(place)].set(low).at[tuple(beside)].set(largest)


def strengthened(values, stream_key, source, target, parts, factor):
    owner, partner = [(jnp.arange(values.shape[position]) // (values.shape[position] // parts)).reshape([-1 if axis == position else 1 for axis in range(values.ndim)]) for position in (source, target)]
    chosen = jax.random.permutation(stream_key, parts)[partner]
    strong = (owner == chosen) | (owner == (partner + parts // 2) % parts)
    return jnp.where(strong, factor * values, values)


def level_of(rng, shape, cuts, low, high):
    level, own = 1.0, jax.random.fold_in(rng, 6)
    for axis_at, shards_of in cuts:
        draws = jnp.exp(jax.random.uniform(jax.random.fold_in(own, axis_at), (shards_of,), jnp.float32, low / len(cuts), high / len(cuts)))
        level = level * jnp.repeat(draws, shape[axis_at] // shards_of).reshape([-1 if axis == axis_at else 1 for axis in range(len(shape))])
    return level


def bell_draw(key, extent, deviation, bound, shards=(), kind=jnp.bfloat16):
    values = deviation * jax.random.normal(key, extent, jnp.float32)
    if shards:
        values = values * level_of(key, extent, shards, -0.22, 0.18)
    return jnp.clip(values, -bound, bound).astype(kind)


def noise_with(stream_key, dims, scale, reach, cuts, heavy, kind=jnp.bfloat16):
    values = scale * jax.random.normal(stream_key, dims, jnp.float32)
    if cuts:
        values = values * level_of(stream_key, dims, cuts, -0.22, 0.18)
    return jnp.clip(strengthened(values, jax.random.fold_in(stream_key, 3), *heavy), -reach, reach).astype(kind)


def setup_inputs(seed: int = 0) -> dict:
    keys = jax.random.split(jax.random.key(seed), 9)
    lower_inverse = draw_lower_inverse(jax.random.fold_in(keys[8], 71), 0)
    coupling = draw_coupling(jax.random.fold_in(keys[8], 71), 0)
    source_cell = place_ends(jax.random.randint(keys[2], (NS,), 0, NB * BW), jax.random.fold_in(keys[2], 1), 0, (NB * BW) - 1).astype(jnp.int32)
    source_wave = bell_draw(keys[3], (NS, 2), 1.0, 6.0, ((0, 64),), jnp.float32)
    inflow_field = bell_draw(keys[4], (NS, 2, BW), 1.0, 6.0, ((0, 64),))
    receiver_cell = place_ends(jax.random.randint(keys[5], (NS, NREC), 0, NB * BW), jax.random.fold_in(keys[5], 1), 0, (NB * BW) - 1).astype(jnp.int32)
    observed = bell_draw(keys[6], (NS, 2, NREC), 1.0, 6.0, ((0, 64),), jnp.float32)
    adjoint = noise_with(keys[7], (NS, NB, 2, BW), 1.0, 16.0, ((0, 64), (1, 8)), (0, 3, 64, 4.0))
    return {"lower_inverse": lower_inverse, "coupling": coupling, "source_cell": source_cell, "source_wave": source_wave, "inflow_field": inflow_field, "receiver_cell": receiver_cell, "observed": observed, "adjoint": adjoint}


def complex_apply(vector, matrix):
    width = matrix.shape[0]
    joined = matrix.reshape(width, 2 * width)
    real_row = jnp.concatenate([vector[:, 0], -vector[:, 1]], axis=1)
    imag_row = jnp.concatenate([vector[:, 1], vector[:, 0]], axis=1)
    stacked = jnp.stack([real_row, imag_row], axis=1).reshape(-1, 2 * width)
    contract_dims = (((1,), (1,)), ((), ()))
    result = lax.dot_general(stacked, joined, contract_dims, preferred_element_type=jnp.float32)
    return result.reshape(vector.shape[0], 2, width)

def reference(lower_inverse, coupling, source_cell, source_wave, inflow_field, receiver_cell, observed, adjoint):
    previous = inflow_field
    blocks = []
    slabs = []
    picked = jnp.zeros(observed.shape, jnp.float32)
    scale = 1.0 / math.sqrt(NS)
    for block in range(NB):
        cell_ids = block * BW + jnp.arange(BW, dtype=jnp.int32)
        hit = source_cell[:, None] == cell_ids[None, :]
        source_term = jnp.where(hit[:, None, :], source_wave[:, :, None], jnp.zeros((), jnp.float32))
        reduced = (source_term - complex_apply(previous, coupling[block])).astype(jnp.bfloat16)
        field = complex_apply(reduced, lower_inverse[block])
        blocks.append(field)
        previous = field.astype(jnp.bfloat16)
        local_ids = receiver_cell - block * BW
        inside = (local_ids >= 0) & (local_ids < BW)
        clipped = jnp.clip(local_ids, 0, BW - 1).astype(jnp.int32)
        index_both = jnp.broadcast_to(clipped[:, None, :], observed.shape)
        values = jnp.take_along_axis(field, index_both, axis=2)
        picked = picked + jnp.where(inside[:, None, :], values, jnp.zeros((), jnp.float32))
        slabs.append(lax.optimization_barrier(jnp.sum(field * adjoint[:, block].astype(jnp.float32), axis=(0, 1))) * scale)
    wavefield = jnp.stack(blocks, axis=1)
    return (wavefield, picked - observed, jnp.stack(slabs, axis=0))
```

```python
import functools
import math

import jax
import jax.numpy as jnp
from jax import lax
from jax.experimental import pallas as pl
from jax.experimental.pallas import tpu as pltpu
from jax.sharding import Mesh, PartitionSpec as P

SRC = ("zh", "y", "x", "c")
CHUNKS = 4
GROUP = 256
LIMIT = 16 << 20
F32, BF16 = jnp.float32, jnp.bfloat16
NT = (((1,), (1,)), ((), ()))


def dot_nt(rows, block):
    return lax.dot_general(rows, block, NT, preferred_element_type=F32)


def group_block(w_ref, group, part, low, high):
    half = group // 2
    tiles = [
        w_ref[c, half, 4 * y + x, part, :, low:high]
        for y in (2 * (group % 2), 2 * (group % 2) + 1)
        for x in range(4)
        for c in range(2)
    ]
    return jnp.concatenate(tiles, axis=0)


def stage_kernel(step, chunks, sc_ref, x_ref, inflow_ref, cells_ref, wave_ref, w_ref, y_ref, field_ref, _w, v_ref):
    owner = sc_ref[0]
    chunk = step - owner
    m, width = x_ref.shape[1], x_ref.shape[2]
    groups = width // GROUP

    @pl.when((chunk >= 0) & (chunk < chunks))
    def _():
        @pl.when(owner == 0)
        def _():
            v_ref[:, 0 : 2 * m] = inflow_ref[...].reshape(1, 2 * m, width)

        @pl.when(owner != 0)
        def _():
            v_ref[:, 0 : 2 * m] = x_ref[...].reshape(1, 2 * m, width)

        straight = v_ref[0]
        crossed = jnp.concatenate([-straight[m:], straight[:m]], axis=0)
        cells = cells_ref[chunk] - owner * width
        waves = wave_ref[chunk]
        lanes = lax.broadcasted_iota(jnp.int32, (m, GROUP), 1)
        reduced = []
        for g in range(groups):
            low = GROUP * g
            acc = dot_nt(straight[:, low:], group_block(w_ref, g, 0, low + GROUP, width + GROUP))
            acc += dot_nt(crossed[:, low:], group_block(w_ref, g, 1, low + GROUP, width + GROUP))
            hit = lanes + low == cells
            term = jnp.concatenate([jnp.where(hit, waves[:, p : p + 1], 0.0) for p in range(2)], axis=0)
            reduced.append((term - acc).astype(BF16))
        straight = jnp.concatenate(reduced, axis=1)
        crossed = jnp.concatenate([-straight[m:], straight[:m]], axis=0)
        for g in range(groups):
            low, high = GROUP * g, GROUP * (g + 1)
            acc = dot_nt(straight[:, :high], group_block(w_ref, g, 0, 0, high))
            acc += dot_nt(crossed[:, :high], group_block(w_ref, g, 1, 0, high))
            acc = acc.reshape(2, m, GROUP)
            field_ref[:, :, low:high] = acc
            y_ref[:, :, low:high] = acc.astype(BF16)


def post_kernel(step, chunks, sc_ref, field_ref, adjoint_ref, cells_ref, _w, _p, _g, wave_out, picked_out, grad_out):
    owner = sc_ref[0]
    chunk = step - owner
    m, width = field_ref.shape[1], field_ref.shape[2]

    @pl.when((chunk >= 0) & (chunk < chunks))
    def _():
        field = field_ref[...]
        wave_out[chunk] = field
        prod = field * adjoint_ref[chunk].astype(F32)
        grad_out[...] += jnp.sum(prod.reshape(2 * m // 8, 8, width), axis=0)
        local = cells_ref[chunk] - owner * width
        tile, lane = local >> 7, local & 127
        for p in range(2):
            got = jnp.zeros((m, 128), F32)
            for t in range(width // 128):
                part = field_ref[p, :, 128 * t : 128 * (t + 1)]
                part = jnp.take_along_axis(part, lane, axis=1, mode="promise_in_bounds")
                got = jnp.where(tile == t, part, got)
            picked_out[chunk, p] = got


def place_kernel(sc_ref, own_ref, own_other_ref, far_ref, far_other_ref, out_ref, sems):
    half, core = sc_ref[1], sc_ref[2]
    pieces = (
        (own_ref, core, half),
        (own_other_ref, 1 - core, half),
        (far_ref, core, 1 - half),
        (far_other_ref, 1 - core, 1 - half),
    )
    copies = [
        pltpu.make_async_copy(ref, out_ref.at[c, h], sems.at[i]) for i, (ref, c, h) in enumerate(pieces)
    ]
    for copy in copies:
        copy.start()
    for copy in copies:
        copy.wait()


def swap(array, axis):
    return lax.ppermute(array, axis, [(0, 1), (1, 0)])


def plane_gather(piece):
    plane = lax.axis_size(("y", "x"))
    spread = jnp.broadcast_to(piece[None], (plane,) + piece.shape)
    return lax.all_to_all(spread, ("y", "x"), 0, 0, tiled=True)


def gather_factor(packed, where):
    far = swap(packed, "zh")
    own = plane_gather(packed)
    own_other = swap(own, "c")
    own, far = lax.optimization_barrier((own, far))
    far = plane_gather(far)
    far_other = swap(far, "c")
    anywhere = pl.BlockSpec(memory_space=pl.ANY)
    return pl.pallas_call(
        place_kernel,
        out_shape=pltpu.VMEM((2, 2) + own.shape, own.dtype),
        in_specs=[pl.BlockSpec(memory_space=pltpu.SMEM)] + [anywhere] * 4,
        out_specs=pl.BlockSpec(memory_space=pltpu.VMEM),
        scratch_shapes=[pltpu.SemaphoreType.DMA((4,))],
        compiler_params=pltpu.CompilerParams(vmem_limit_bytes=LIMIT),
        name="place",
    )(where, own, own_other, far, far_other)


def per_device(lower, coupling, source_cell, source_wave, inflow, receiver_cell, observed, adjoint):
    owner = lax.axis_index("fac")
    stages = lax.axis_size("fac")
    src = lax.axis_index(SRC)
    width = lower.shape[3]
    rows = lower.shape[1]
    sources = source_cell.shape[0]
    m = sources // CHUNKS

    split = (src // (GROUP // rows) + 1) * GROUP
    low = jnp.pad(lower[0].transpose(1, 0, 2), ((0, 0), (0, 0), (0, GROUP)))
    high = jnp.pad(coupling[0].transpose(1, 0, 2), ((0, 0), (0, 0), (GROUP, 0)))
    packed = jnp.where(lax.broadcasted_iota(jnp.int32, low.shape, 2) < split, low, high)
    where = jnp.stack([owner, lax.axis_index("zh"), lax.axis_index("c")])
    factor = gather_factor(packed, where)

    def by_chunk(array):
        return array.reshape((CHUNKS, m) + array.shape[1:])

    inflow = by_chunk(inflow).transpose(0, 2, 1, 3)
    adjoint = by_chunk(adjoint[:, 0]).transpose(0, 2, 1, 3)
    observed = by_chunk(observed).transpose(0, 2, 1, 3)
    cells, waves, receivers = by_chunk(source_cell[:, None]), by_chunk(source_wave), by_chunk(receiver_cell)

    vmem = pl.BlockSpec(memory_space=pltpu.VMEM)
    smem = pl.BlockSpec(memory_space=pltpu.SMEM)
    stage = lambda t: pl.pallas_call(
        functools.partial(stage_kernel, t, CHUNKS),
        out_shape=(
            pltpu.VMEM((2, m, width), BF16),
            pltpu.VMEM((2, m, width), F32),
            pltpu.VMEM(factor.shape, BF16),
        ),
        in_specs=[smem] + [vmem] * 5,
        out_specs=(vmem, vmem, vmem),
        input_output_aliases={5: 2},
        scratch_shapes=[pltpu.VMEM((1, 2 * m, width), BF16)],
        cost_estimate=pl.CostEstimate(
            flops=int(2 * 2 * 2 * m * 2 * width * width * 0.625),
            bytes_accessed=4 * width * (width + GROUP),
            transcendentals=0,
        ),
        compiler_params=pltpu.CompilerParams(vmem_limit_bytes=LIMIT),
        name="stage",
    )
    post = lambda t: pl.pallas_call(
        functools.partial(post_kernel, t, CHUNKS),
        out_shape=(
            pltpu.VMEM((CHUNKS, 2, m, width), F32),
            pltpu.VMEM((CHUNKS, 2, m, receivers.shape[2]), F32),
            pltpu.VMEM((8, width), F32),
        ),
        in_specs=[smem] + [vmem] * 6,
        out_specs=(vmem, vmem, vmem),
        input_output_aliases={4: 0, 5: 1, 6: 2},
        cost_estimate=pl.CostEstimate(flops=8 * m * width, bytes_accessed=24 * m * width, transcendentals=0),
        compiler_params=pltpu.CompilerParams(vmem_limit_bytes=LIMIT),
        name="post",
    )
    field_all = jnp.zeros((CHUNKS, 2, m, width), F32)
    picked = jnp.zeros((CHUNKS, 2, m, receivers.shape[2]), F32)
    grad = jnp.zeros((8, width), F32)
    x = jnp.zeros((2, m, width), BF16)
    steps = CHUNKS + stages - 1
    for t in range(steps):
        y, field, factor = stage(t)(where, x, inflow[min(t, CHUNKS - 1)], cells, waves, factor)
        pairs = [(i, i + 1) for i in range(stages - 1) if 0 <= t - i < CHUNKS]
        if pairs:
            x = lax.ppermute(y, "fac", pairs)
        field_all, picked, grad = post(t)(where, field, adjoint, receivers, field_all, picked, grad)
        x, field_all, picked, grad = lax.optimization_barrier((x, field_all, picked, grad))

    picked = picked.astype(BF16)
    step = stages // 2
    while step:
        picked = picked + lax.ppermute(picked, "fac", [(i, i ^ step) for i in range(stages)])
        step //= 2
    residual = (picked.astype(F32) - observed).transpose(0, 2, 1, 3).reshape(sources, 2, -1)
    shards = lax.axis_size(SRC)
    scale = 1.0 / math.sqrt(sources * shards)
    terms = (jnp.sum(grad, axis=0) * scale).reshape(shards, rows)
    terms = lax.all_to_all(terms, SRC, 0, 0, tiled=True)
    gradient = jnp.sum(terms, axis=0)[None]
    wavefield = field_all.transpose(0, 2, 1, 3).reshape(sources, 1, 2, width)
    return wavefield, residual, gradient


def solution(mesh):
    grid = Mesh(mesh.devices.reshape(2, 4, 4, 2, -1), SRC + ("fac",))
    placed = (
        P("fac", SRC, None, None),
        P("fac", SRC, None, None),
        P(SRC),
        P(SRC, None),
        P(SRC, None, None),
        P(SRC, None),
        P(SRC, None, None),
        P(SRC, "fac", None, None),
    )
    return jax.shard_map(
        per_device,
        mesh=grid,
        in_specs=placed,
        out_specs=(P(SRC, "fac", None, None), P(SRC, None, None), P("fac", SRC)),
        check_vma=False,
    )
```

```python
import functools
import math

import jax
import jax.numpy as jnp
from jax import lax
from jax.experimental import pallas as pl
from jax.experimental.pallas import tpu as pltpu
from jax.sharding import Mesh, PartitionSpec as P

SRC = ("zh", "y", "x", "c")
CHUNKS = 4
GROUP = 256
LIMIT = 16 << 20
F32, BF16 = jnp.float32, jnp.bfloat16
NT = (((1,), (1,)), ((), ()))


def dot_nt(rows, block):
    return lax.dot_general(rows, block, NT, preferred_element_type=F32)


def group_block(w_ref, group, part, low, high):
    half = group // 2
    tiles = [
        w_ref[c, half, 4 * y + x, part, :, low:high]
        for y in (2 * (group % 2), 2 * (group % 2) + 1)
        for x in range(4)
        for c in range(2)
    ]
    return jnp.concatenate(tiles, axis=0)


def stage_kernel(step, chunks, stages, sc_ref, x_ref, inflow_ref, cells_ref, wave_ref, receivers_ref, w_ref, _p, y_ref, field_ref, _w, picked_ref, v_ref):
    owner = sc_ref[0]
    chunk = step - owner
    m, width = inflow_ref.shape[1], inflow_ref.shape[2]
    groups = width // GROUP

    @pl.when((chunk >= 0) & (chunk < chunks))
    def _():
        @pl.when(owner == 0)
        def _():
            v_ref[...] = inflow_ref[...].reshape(1, 2 * m, width)
            picked_ref[chunk] = jnp.zeros(picked_ref.shape[1:], BF16)

        @pl.when(owner != 0)
        def _():
            v_ref[...] = x_ref[:, :, :width].reshape(1, 2 * m, width)
            picked_ref[chunk] = x_ref[:, :, width:]

        straight = v_ref[0]
        crossed = jnp.concatenate([-straight[m:], straight[:m]], axis=0)
        cells = cells_ref[chunk] - owner * width
        waves = wave_ref[chunk]
        lanes = lax.broadcasted_iota(jnp.int32, (m, GROUP), 1)
        reduced = []
        for g in range(groups):
            low = GROUP * g
            acc = dot_nt(straight[:, low:], group_block(w_ref, g, 0, low + GROUP, width + GROUP))
            acc += dot_nt(crossed[:, low:], group_block(w_ref, g, 1, low + GROUP, width + GROUP))
            hit = lanes + low == cells
            term = jnp.concatenate([jnp.where(hit, waves[:, p : p + 1], 0.0) for p in range(2)], axis=0)
            reduced.append((term - acc).astype(BF16))
        straight = jnp.concatenate(reduced, axis=1)
        crossed = jnp.concatenate([-straight[m:], straight[:m]], axis=0)
        for g in range(groups):
            low, high = GROUP * g, GROUP * (g + 1)
            acc = dot_nt(straight[:, :high], group_block(w_ref, g, 0, 0, high))
            acc += dot_nt(crossed[:, :high], group_block(w_ref, g, 1, 0, high))
            acc = acc.reshape(2, m, GROUP)
            field_ref[:, :, low:high] = acc
            y_ref[:, :, low:high] = acc.astype(BF16)
        local = receivers_ref[chunk] - owner * width
        tile, lane = local >> 7, local & 127
        for p in range(2):
            got = jnp.zeros((m, 128), F32)
            for t in range(width // 128):
                part = field_ref[p, :, 128 * t : 128 * (t + 1)]
                part = jnp.take_along_axis(part, lane, axis=1, mode="promise_in_bounds")
                got = jnp.where(tile == t, part, got)
            total = picked_ref[chunk, p] + got.astype(BF16)
            picked_ref[chunk, p] = total
            y_ref[p, :, width:] = total

    if step == chunks + stages - 2:
        @pl.when(owner != stages - 1)
        def _():
            picked_ref[...] = jnp.zeros_like(picked_ref)


def post_kernel(step, chunks, sc_ref, field_ref, adjoint_ref, _w, _g, wave_out, grad_out):
    owner = sc_ref[0]
    chunk = step - owner
    m, width = field_ref.shape[1], field_ref.shape[2]

    @pl.when((chunk >= 0) & (chunk < chunks))
    def _():
        field = field_ref[...]
        wave_out[chunk] = field
        prod = field * adjoint_ref[chunk].astype(F32)
        grad_out[...] += jnp.sum(prod.reshape(2 * m // 8, 8, width), axis=0)


def place_kernel(sc_ref, own_ref, own_other_ref, far_ref, far_other_ref, out_ref, sems):
    half, core = sc_ref[1], sc_ref[2]
    pieces = (
        (own_ref, core, half),
        (own_other_ref, 1 - core, half),
        (far_ref, core, 1 - half),
        (far_other_ref, 1 - core, 1 - half),
    )
    copies = [
        pltpu.make_async_copy(ref, out_ref.at[c, h], sems.at[i]) for i, (ref, c, h) in enumerate(pieces)
    ]
    for copy in copies:
        copy.start()
    for copy in copies:
        copy.wait()


def swap(array, axis):
    return lax.ppermute(array, axis, [(0, 1), (1, 0)])


def plane_gather(piece):
    plane = lax.axis_size(("y", "x"))
    spread = jnp.broadcast_to(piece[None], (plane,) + piece.shape)
    return lax.all_to_all(spread, ("y", "x"), 0, 0, tiled=True)


def gather_factor(packed, where, inflow):
    far = swap(packed, "zh")
    packed, inflow = lax.optimization_barrier((packed, inflow))
    own = plane_gather(packed)
    own_other = swap(own, "c")
    far = plane_gather(far)
    far_other = swap(far, "c")
    anywhere = pl.BlockSpec(memory_space=pl.ANY)
    return pl.pallas_call(
        place_kernel,
        out_shape=pltpu.VMEM((2, 2) + own.shape, own.dtype),
        in_specs=[pl.BlockSpec(memory_space=pltpu.SMEM)] + [anywhere] * 4,
        out_specs=pl.BlockSpec(memory_space=pltpu.VMEM),
        scratch_shapes=[pltpu.SemaphoreType.DMA((4,))],
        compiler_params=pltpu.CompilerParams(vmem_limit_bytes=LIMIT),
        name="place",
    )(where, own, own_other, far, far_other), inflow


def fan_out(stages):
    last = stages - 1
    if stages != 8:
        return [[[(last, i)] for i in range(last)]]
    return [[[(7, 3)], [(7, 5)]], [[(3, 1), (5, 4)]], [[(3, 2), (5, 6), (1, 0)]]]


def per_device(lower, coupling, source_cell, source_wave, inflow, receiver_cell, observed, adjoint):
    owner = lax.axis_index("fac")
    stages = lax.axis_size("fac")
    src = lax.axis_index(SRC)
    width = lower.shape[3]
    rows = lower.shape[1]
    sources = source_cell.shape[0]
    m = sources // CHUNKS

    split = (src // (GROUP // rows) + 1) * GROUP
    low = jnp.pad(lower[0].transpose(1, 0, 2), ((0, 0), (0, 0), (0, GROUP)))
    high = jnp.pad(coupling[0].transpose(1, 0, 2), ((0, 0), (0, 0), (GROUP, 0)))
    packed = jnp.where(lax.broadcasted_iota(jnp.int32, low.shape, 2) < split, low, high)
    where = jnp.stack([owner, lax.axis_index("zh"), lax.axis_index("c")])

    def by_chunk(array):
        return array.reshape((CHUNKS, m) + array.shape[1:])

    inflow = by_chunk(inflow).transpose(0, 2, 1, 3)
    factor, inflow = gather_factor(packed, where, inflow)
    adjoint = by_chunk(adjoint[:, 0]).transpose(0, 2, 1, 3)
    observed = by_chunk(observed).transpose(0, 2, 1, 3)
    cells, waves, receivers = by_chunk(source_cell[:, None]), by_chunk(source_wave), by_chunk(receiver_cell)

    vmem = pl.BlockSpec(memory_space=pltpu.VMEM)
    smem = pl.BlockSpec(memory_space=pltpu.SMEM)
    stage = lambda t: pl.pallas_call(
        functools.partial(stage_kernel, t, CHUNKS, stages),
        out_shape=(
            pltpu.VMEM((2, m, width + 128), BF16),
            pltpu.VMEM((2, m, width), F32),
            pltpu.VMEM(factor.shape, BF16),
            pltpu.VMEM((CHUNKS, 2, m, 128), BF16),
        ),
        in_specs=[smem] + [vmem] * 7,
        out_specs=(vmem, vmem, vmem, vmem),
        input_output_aliases={6: 2, 7: 3},
        scratch_shapes=[pltpu.VMEM((1, 2 * m, width), BF16)],
        cost_estimate=pl.CostEstimate(
            flops=int(2 * 2 * 2 * m * 2 * width * width * 0.625),
            bytes_accessed=4 * width * (width + GROUP),
            transcendentals=0,
        ),
        compiler_params=pltpu.CompilerParams(vmem_limit_bytes=LIMIT),
        name="stage",
    )
    post = lambda t: pl.pallas_call(
        functools.partial(post_kernel, t, CHUNKS),
        out_shape=(
            pltpu.VMEM((CHUNKS, 2, m, width), F32),
            pltpu.VMEM((8, width), F32),
        ),
        in_specs=[smem] + [vmem] * 4,
        out_specs=(vmem, vmem),
        input_output_aliases={3: 0, 4: 1},
        cost_estimate=pl.CostEstimate(flops=8 * m * width, bytes_accessed=24 * m * width, transcendentals=0),
        compiler_params=pltpu.CompilerParams(vmem_limit_bytes=LIMIT),
        name="post",
    )
    field_all = jnp.zeros((CHUNKS, 2, m, width), F32)
    picked = jnp.zeros((CHUNKS, 2, m, receivers.shape[2]), BF16)
    grad = jnp.zeros((8, width), F32)
    x = jnp.zeros((2, m, width + 128), BF16)
    for t in range(CHUNKS + stages - 1):
        y, field, factor, picked = stage(t)(
            where, x, inflow[min(t, CHUNKS - 1)], cells, waves, receivers, factor, picked
        )
        pairs = [(i, i + 1) for i in range(stages - 1) if 0 <= t - i < CHUNKS]
        if pairs:
            x = lax.ppermute(y, "fac", pairs)
        field_all, grad = post(t)(where, field, adjoint, field_all, grad)
        x, field_all, grad = lax.optimization_barrier((x, field_all, grad))

    rounds = fan_out(stages)
    first = [lax.ppermute(picked, "fac", pairs) for pairs in rounds[0]]
    shards = lax.axis_size(SRC)
    scale = 1.0 / math.sqrt(sources * shards)
    terms = (jnp.sum(grad, axis=0) * scale).reshape(shards, rows)
    terms = lax.all_to_all(terms, SRC, 0, 0, tiled=True)
    first, terms = lax.optimization_barrier((first, terms))
    gradient = jnp.sum(terms, axis=0)[None]
    picked = functools.reduce(jnp.add, first, picked)
    for pairs in rounds[1:]:
        picked = picked + lax.ppermute(picked, "fac", pairs[0])
    residual = (picked.astype(F32) - observed).transpose(0, 2, 1, 3).reshape(sources, 2, -1)
    wavefield = field_all.transpose(0, 2, 1, 3).reshape(sources, 1, 2, width)
    return wavefield, residual, gradient


def solution(mesh):
    grid = Mesh(mesh.devices.reshape(2, 4, 4, 2, -1), SRC + ("fac",))
    placed = (
        P("fac", SRC, None, None),
        P("fac", SRC, None, None),
        P(SRC),
        P(SRC, None),
        P(SRC, None, None),
        P(SRC, None),
        P(SRC, None, None),
        P(SRC, "fac", None, None),
    )
    return jax.shard_map(
        per_device,
        mesh=grid,
        in_specs=placed,
        out_specs=(P(SRC, "fac", None, None), P(SRC, None, None), P("fac", SRC)),
        check_vma=False,
    )
```

```python
import functools
import math

import jax
import jax.numpy as jnp
from jax import lax
from jax.experimental import pallas as pl
from jax.experimental.pallas import tpu as pltpu
from jax.sharding import Mesh, PartitionSpec as P

SRC = ("zh", "y", "x", "c")
CHUNKS = 4
GROUP = 256
LIMIT = 16 << 20
SPLIT = 4
F32, BF16 = jnp.float32, jnp.bfloat16
NT = (((1,), (1,)), ((), ()))


def dot_nt(rows, block):
    return lax.dot_general(rows, block, NT, preferred_element_type=F32)


def group_block(w_ref, group, part, low, high):
    half = group // 2
    tiles = [
        w_ref[c, half, 4 * y + x, part, :, low:high]
        for y in (2 * (group % 2), 2 * (group % 2) + 1)
        for x in range(4)
        for c in range(2)
    ]
    return jnp.concatenate(tiles, axis=0)


def stage_kernel(step, chunks, stages, sc_ref, x_ref, inflow_ref, cells_ref, wave_ref, receivers_ref, w_ref, _p, field_ref, _w, picked_ref, *rest):
    v_ref = rest[-1]
    last = step == chunks + stages - 2
    owner = sc_ref[0]
    chunk = step - owner
    m, width = inflow_ref.shape[1], inflow_ref.shape[2]
    groups = width // GROUP

    @pl.when((chunk >= 0) & (chunk < chunks))
    def _():
        @pl.when(owner == 0)
        def _():
            v_ref[...] = inflow_ref[...].reshape(1, 2 * m, width)
            picked_ref[chunk] = jnp.zeros(picked_ref.shape[1:], BF16)

        @pl.when(owner != 0)
        def _():
            v_ref[...] = x_ref[:, :, :width].reshape(1, 2 * m, width)
            picked_ref[chunk] = x_ref[:, :, width:]

        straight = v_ref[0]
        crossed = jnp.concatenate([-straight[m:], straight[:m]], axis=0)
        cells = cells_ref[chunk] - owner * width
        waves = wave_ref[chunk]
        lanes = lax.broadcasted_iota(jnp.int32, (m, GROUP), 1)
        reduced = []
        for g in range(groups):
            low = GROUP * g
            acc = dot_nt(straight[:, low:], group_block(w_ref, g, 0, low + GROUP, width + GROUP))
            acc += dot_nt(crossed[:, low:], group_block(w_ref, g, 1, low + GROUP, width + GROUP))
            hit = lanes + low == cells
            term = jnp.concatenate([jnp.where(hit, waves[:, p : p + 1], 0.0) for p in range(2)], axis=0)
            reduced.append((term - acc).astype(BF16))
        straight = jnp.concatenate(reduced, axis=1)
        crossed = jnp.concatenate([-straight[m:], straight[:m]], axis=0)
        for g in range(groups):
            low, high = GROUP * g, GROUP * (g + 1)
            acc = dot_nt(straight[:, :high], group_block(w_ref, g, 0, 0, high))
            acc += dot_nt(crossed[:, :high], group_block(w_ref, g, 1, 0, high))
            acc = acc.reshape(2, m, GROUP)
            field_ref[:, :, low:high] = acc
            if not last:
                rest[0][:, :, low:high] = acc.astype(BF16)
        local = receivers_ref[chunk] - owner * width
        tile, lane = local >> 7, local & 127
        for p in range(2):
            got = jnp.zeros((m, 128), F32)
            for t in range(width // 128):
                part = field_ref[p, :, 128 * t : 128 * (t + 1)]
                part = jnp.take_along_axis(part, lane, axis=1, mode="promise_in_bounds")
                got = jnp.where(tile == t, part, got)
            total = picked_ref[chunk, p] + got.astype(BF16)
            picked_ref[chunk, p] = total
            if not last:
                rest[0][p, :, width:] = total

    if last:
        @pl.when(owner != stages - 1)
        def _():
            picked_ref[...] = jnp.zeros_like(picked_ref)


def post_kernel(step, chunks, sc_ref, field_ref, adjoint_ref, *refs):
    wave_out, grad_out, rows_ref, sem = refs[-4:]
    owner = sc_ref[0]
    chunk = step - owner
    m, width = field_ref.shape[1], field_ref.shape[2]

    if step == 0:
        grad_out[...] = jnp.zeros_like(grad_out)

    @pl.when((chunk >= 0) & (chunk < chunks))
    def _():
        field = field_ref[...]
        for p in range(2):
            rows_ref[:, p, :] = field[p]
        store = pltpu.make_async_copy(rows_ref, wave_out.at[pl.ds(chunk * m, m)], sem)
        store.start()
        prod = field * adjoint_ref[chunk].astype(F32)
        grad_out[...] += jnp.sum(prod.reshape(2 * m // 8, 8, width), axis=0)
        store.wait()


def place_kernel(sc_ref, own_ref, own_other_ref, far_ref, far_other_ref, out_ref, sems):
    half, core = sc_ref[1], sc_ref[2]
    pieces = (
        (own_ref, core, half),
        (own_other_ref, 1 - core, half),
        (far_ref, core, 1 - half),
        (far_other_ref, 1 - core, 1 - half),
    )
    part = own_ref.shape[0] // SPLIT
    copies = [
        pltpu.make_async_copy(
            ref.at[pl.ds(part * k, part)], out_ref.at[c, h, pl.ds(part * k, part)], sems.at[i, k]
        )
        for i, (ref, c, h) in enumerate(pieces)
        for k in range(SPLIT)
    ]
    for copy in copies:
        copy.start()
    for copy in copies:
        copy.wait()


def swap(array, axis):
    return lax.ppermute(array, axis, [(0, 1), (1, 0)])


def plane_gather(piece):
    plane = lax.axis_size(("y", "x"))
    spread = jnp.broadcast_to(piece[None], (plane,) + piece.shape)
    return lax.all_to_all(spread, ("y", "x"), 0, 0, tiled=True)


def empty_plane(piece):
    return jnp.zeros((lax.axis_size(("y", "x")),) + piece.shape, piece.dtype)


def gather_factor(packed, where):
    far = swap(packed, "zh")
    own = lax.cond(where[0] < lax.axis_size("fac"), plane_gather, empty_plane, packed)
    own_other = swap(own, "c")
    far = plane_gather(far)
    far_other = swap(far, "c")
    anywhere = pl.BlockSpec(memory_space=pl.ANY)
    return pl.pallas_call(
        place_kernel,
        out_shape=pltpu.VMEM((2, 2) + own.shape, own.dtype),
        in_specs=[pl.BlockSpec(memory_space=pltpu.SMEM)] + [anywhere] * 4,
        out_specs=pl.BlockSpec(memory_space=pltpu.VMEM),
        scratch_shapes=[pltpu.SemaphoreType.DMA((4, SPLIT))],
        compiler_params=pltpu.CompilerParams(vmem_limit_bytes=LIMIT),
        name="place",
    )(where, own, own_other, far, far_other)


def fan_out(stages):
    last = stages - 1
    if stages != 8:
        return [[[(last, i)] for i in range(last)]]
    return [[[(7, 3)]], [[(3, 1)], [(3, 5)]], [[(3, 2), (5, 6), (1, 0)], [(3, 4)]]]


def per_device(lower, coupling, source_cell, source_wave, inflow, receiver_cell, observed, adjoint):
    owner = lax.axis_index("fac")
    stages = lax.axis_size("fac")
    src = lax.axis_index(SRC)
    width = lower.shape[3]
    rows = lower.shape[1]
    sources = source_cell.shape[0]
    m = sources // CHUNKS

    split = (src // (GROUP // rows) + 1) * GROUP
    low = jnp.pad(lower[0].transpose(1, 0, 2), ((0, 0), (0, 0), (0, GROUP)))
    high = jnp.pad(coupling[0].transpose(1, 0, 2), ((0, 0), (0, 0), (GROUP, 0)))
    packed = jnp.where(lax.broadcasted_iota(jnp.int32, low.shape, 2) < split, low, high)
    where = jnp.stack([owner, lax.axis_index("zh"), lax.axis_index("c")])

    def by_chunk(array):
        return array.reshape((CHUNKS, m) + array.shape[1:])

    inflow = by_chunk(inflow).transpose(0, 2, 1, 3)
    factor = gather_factor(packed, where)
    adjoint = by_chunk(adjoint[:, 0]).transpose(0, 2, 1, 3)
    observed = by_chunk(observed).transpose(0, 2, 1, 3)
    cells, waves, receivers = by_chunk(source_cell[:, None]), by_chunk(source_wave), by_chunk(receiver_cell)

    steps = CHUNKS + stages - 1
    vmem = pl.BlockSpec(memory_space=pltpu.VMEM)
    smem = pl.BlockSpec(memory_space=pltpu.SMEM)
    stage = lambda t: pl.pallas_call(
        functools.partial(stage_kernel, t, CHUNKS, stages),
        out_shape=(
            pltpu.VMEM((2, m, width), F32),
            pltpu.VMEM(factor.shape, BF16),
            pltpu.VMEM((CHUNKS, 2, m, 128), BF16),
        )
        + ((pltpu.VMEM((2, m, width + 128), BF16),) if t < steps - 1 else ()),
        in_specs=[smem] + [vmem] * 7,
        out_specs=(vmem,) * (4 if t < steps - 1 else 3),
        input_output_aliases={6: 1, 7: 2},
        scratch_shapes=[pltpu.VMEM((1, 2 * m, width), BF16)],
        cost_estimate=pl.CostEstimate(
            flops=int(2 * 2 * 2 * m * 2 * width * width * 0.625),
            bytes_accessed=4 * width * (width + GROUP),
            transcendentals=0,
        ),
        compiler_params=pltpu.CompilerParams(vmem_limit_bytes=LIMIT),
        name="stage",
    )
    post = lambda t: pl.pallas_call(
        functools.partial(post_kernel, t, CHUNKS),
        out_shape=(
            jax.ShapeDtypeStruct((sources, 2, width), F32),
            pltpu.VMEM((8, width), F32),
        ),
        in_specs=[smem, vmem, vmem] + ([pl.BlockSpec(memory_space=pl.ANY), vmem] if t else []),
        out_specs=(pl.BlockSpec(memory_space=pl.ANY), vmem),
        scratch_shapes=[pltpu.VMEM((m, 2, width), F32), pltpu.SemaphoreType.DMA(())],
        input_output_aliases={3: 0, 4: 1} if t else {},
        compiler_params=pltpu.CompilerParams(vmem_limit_bytes=LIMIT),
        cost_estimate=pl.CostEstimate(flops=8 * m * width, bytes_accessed=24 * m * width, transcendentals=0),
        name="post",
    )
    picked = jnp.zeros((CHUNKS, 2, m, receivers.shape[2]), BF16)
    done = ()
    x = jnp.zeros((2, m, width + 128), BF16)
    for t in range(steps):
        field, factor, picked, *y = stage(t)(
            where, x, inflow[min(t, CHUNKS - 1)], cells, waves, receivers, factor, picked
        )
        pairs = [(i, i + 1) for i in range(stages - 1) if 0 <= t - i < CHUNKS]
        if pairs:
            x = lax.ppermute(y[0], "fac", pairs)
        done = post(t)(where, field, adjoint, *done)
        x, done = lax.optimization_barrier((x, done))
    wavefield, grad = done

    rounds = fan_out(stages)
    first = [lax.ppermute(picked, "fac", pairs) for pairs in rounds[0]]
    shards = lax.axis_size(SRC)
    scale = 1.0 / math.sqrt(sources * shards)
    terms = (jnp.sum(grad, axis=0) * scale).reshape(shards, rows)
    terms = lax.all_to_all(terms, SRC, 0, 0, tiled=True)
    first, terms = lax.optimization_barrier((first, terms))
    gradient = jnp.sum(terms, axis=0)[None]
    picked = functools.reduce(jnp.add, first, picked)
    for pairs in rounds[1:]:
        picked = functools.reduce(jnp.add, [lax.ppermute(picked, "fac", p) for p in pairs], picked)
    residual = (picked.astype(F32) - observed).transpose(0, 2, 1, 3).reshape(sources, 2, -1)
    return wavefield[:, None], residual, gradient


def solution(mesh):
    grid = Mesh(mesh.devices.reshape(2, 4, 4, 2, -1), SRC + ("fac",))
    placed = (
        P("fac", SRC, None, None),
        P("fac", SRC, None, None),
        P(SRC),
        P(SRC, None),
        P(SRC, None, None),
        P(SRC, None),
        P(SRC, None, None),
        P(SRC, "fac", None, None),
    )
    return jax.shard_map(
        per_device,
        mesh=grid,
        in_specs=placed,
        out_specs=(P(SRC, "fac", None, None), P(SRC, None, None), P("fac", SRC)),
        check_vma=False,
    )
```

```python
import functools
import math

import jax
import jax.numpy as jnp
from jax import lax
from jax.experimental import pallas as pl
from jax.experimental.pallas import tpu as pltpu
from jax.sharding import Mesh, PartitionSpec as P

SRC = ("zh", "y", "x", "c")
CHUNKS = 4
GROUP = 128
LIMIT = 16 << 20
SPLIT = 4
F32, BF16 = jnp.float32, jnp.bfloat16
NT = (((1,), (1,)), ((), ()))
NN = (((1,), (0,)), ((), ()))


def multiply(block, columns, dims):
    return lax.dot_general(block, columns, dims, preferred_element_type=F32)


def group_block(w_ref, group, part, low, high):
    tiles = [w_ref[c, group // 4, 4 * (group % 4) + x, part, :, low:high] for x in range(4) for c in range(2)]
    return jnp.concatenate(tiles, axis=0)


def stage_kernel(
    step, chunks, stages, sc_ref, x_ref, inflow_ref, cells_ref, wave_ref, receivers_ref, w_ref, _p,
    field_ref, _w, picked_ref, *rest
):
    v_ref = rest[-1]
    last = step == chunks + stages - 2
    owner = sc_ref[0]
    chunk = step - owner
    m, width = inflow_ref.shape[1], inflow_ref.shape[2]
    groups = width // GROUP

    @pl.when((chunk >= 0) & (chunk < chunks))
    def _():
        @pl.when(owner == 0)
        def _():
            v_ref[...] = inflow_ref[...].reshape(1, 2 * m, width)
            picked_ref[chunk] = jnp.zeros(picked_ref.shape[1:], BF16)

        @pl.when(owner != 0)
        def _():
            v_ref[...] = x_ref[:, :, :width].reshape(1, 2 * m, width)
            picked_ref[chunk] = x_ref[:, :, width:]

        straight = v_ref[0]
        crossed = jnp.concatenate([-straight[m:], straight[:m]], axis=0)
        cells = cells_ref[chunk] - owner * width
        waves = wave_ref[chunk]
        rows = lax.broadcasted_iota(jnp.int32, (GROUP, 2 * m), 0)
        reduced, turned = [], []
        for g in range(groups):
            low = GROUP * g
            acc = multiply(group_block(w_ref, g, 0, low + GROUP, width + GROUP), straight[:, low:], NT)
            acc += multiply(group_block(w_ref, g, 1, low + GROUP, width + GROUP), crossed[:, low:], NT)
            value = jnp.where(rows + low == cells, waves, 0.0) - acc
            reduced.append(value.astype(BF16))
            turned.append(jnp.concatenate([-value[:, m:], value[:, :m]], axis=1).astype(BF16))
        reduced, turned = jnp.concatenate(reduced, axis=0), jnp.concatenate(turned, axis=0)
        for g in range(groups):
            low, high = GROUP * g, GROUP * (g + 1)
            acc = multiply(group_block(w_ref, g, 0, 0, high), reduced[:high], NN)
            acc += multiply(group_block(w_ref, g, 1, 0, high), turned[:high], NN)
            acc = acc.T.reshape(2, m, GROUP)
            field_ref[:, :, low:high] = acc
            if not last:
                rest[0][:, :, low:high] = acc.astype(BF16)
        local = receivers_ref[chunk] - owner * width
        tile, lane = local >> 7, local & 127
        for p in range(2):
            got = jnp.zeros((m, 128), F32)
            for t in range(width // 128):
                part = field_ref[p, :, 128 * t : 128 * (t + 1)]
                part = jnp.take_along_axis(part, lane, axis=1, mode="promise_in_bounds")
                got = jnp.where(tile == t, part, got)
            total = picked_ref[chunk, p] + got.astype(BF16)
            picked_ref[chunk, p] = total
            if not last:
                rest[0][p, :, width:] = total

    if last:
        @pl.when(owner != stages - 1)
        def _():
            picked_ref[...] = jnp.zeros_like(picked_ref)


def post_kernel(step, chunks, sc_ref, field_ref, adjoint_ref, *refs):
    wave_out, grad_out, rows_ref, sem = refs[-4:]
    owner = sc_ref[0]
    chunk = step - owner
    m, width = field_ref.shape[1], field_ref.shape[2]

    if step == 0:
        grad_out[...] = jnp.zeros_like(grad_out)

    @pl.when((chunk >= 0) & (chunk < chunks))
    def _():
        field = field_ref[...]
        for p in range(2):
            rows_ref[:, p, :] = field[p]
        store = pltpu.make_async_copy(rows_ref, wave_out.at[pl.ds(chunk * m, m)], sem)
        store.start()
        prod = field * adjoint_ref[chunk].astype(F32)
        grad_out[...] += jnp.sum(prod.reshape(2 * m // 8, 8, width), axis=0)
        store.wait()


def place_kernel(sc_ref, own_ref, own_other_ref, far_ref, far_other_ref, out_ref, sems):
    half, core = sc_ref[1], sc_ref[2]
    pieces = (
        (own_ref, core, half),
        (own_other_ref, 1 - core, half),
        (far_ref, core, 1 - half),
        (far_other_ref, 1 - core, 1 - half),
    )
    part = own_ref.shape[0] // SPLIT
    copies = [
        pltpu.make_async_copy(
            ref.at[pl.ds(part * k, part)], out_ref.at[c, h, pl.ds(part * k, part)], sems.at[i, k]
        )
        for i, (ref, c, h) in enumerate(pieces)
        for k in range(SPLIT)
    ]
    for copy in copies:
        copy.start()
    for copy in copies:
        copy.wait()


def swap(array, axis):
    return lax.ppermute(array, axis, [(0, 1), (1, 0)])


def plane_gather(piece):
    plane = lax.axis_size(("y", "x"))
    spread = jnp.broadcast_to(piece[None], (plane,) + piece.shape)
    return lax.all_to_all(spread, ("y", "x"), 0, 0, tiled=True)


def gather_factor(packed, where):
    far = swap(packed, "zh")
    own = plane_gather(packed)
    own_other = swap(own, "c")
    far = plane_gather(far)
    far_other = swap(far, "c")
    anywhere = pl.BlockSpec(memory_space=pl.ANY)
    return pl.pallas_call(
        place_kernel,
        out_shape=pltpu.VMEM((2, 2) + own.shape, own.dtype),
        in_specs=[pl.BlockSpec(memory_space=pltpu.SMEM)] + [anywhere] * 4,
        out_specs=pl.BlockSpec(memory_space=pltpu.VMEM),
        scratch_shapes=[pltpu.SemaphoreType.DMA((4, SPLIT))],
        compiler_params=pltpu.CompilerParams(vmem_limit_bytes=LIMIT),
        name="place",
    )(where, own, own_other, far, far_other)


def fan_out(stages):
    last = stages - 1
    if stages != 8:
        return [[[(last, i)] for i in range(last)]]
    return [[[(7, 3)]], [[(3, 1)], [(3, 5)]], [[(3, 2), (5, 6), (1, 0)], [(3, 4)]]]


def per_device(lower, coupling, source_cell, source_wave, inflow, receiver_cell, observed, adjoint):
    owner = lax.axis_index("fac")
    stages = lax.axis_size("fac")
    src = lax.axis_index(SRC)
    width = lower.shape[3]
    rows = lower.shape[1]
    sources = source_cell.shape[0]
    m = sources // CHUNKS

    split = (src // (GROUP // rows) + 1) * GROUP
    low = jnp.pad(lower[0].transpose(1, 0, 2), ((0, 0), (0, 0), (0, GROUP)))
    high = jnp.pad(coupling[0].transpose(1, 0, 2), ((0, 0), (0, 0), (GROUP, 0)))
    packed = jnp.where(lax.broadcasted_iota(jnp.int32, low.shape, 2) < split, low, high)
    where = jnp.stack([owner, lax.axis_index("zh"), lax.axis_index("c")])

    def by_chunk(array):
        return array.reshape((CHUNKS, m) + array.shape[1:])

    inflow = by_chunk(inflow).transpose(0, 2, 1, 3)
    factor = gather_factor(packed, where)
    adjoint = by_chunk(adjoint[:, 0]).transpose(0, 2, 1, 3)
    observed = by_chunk(observed).transpose(0, 2, 1, 3)
    cells = jnp.tile(by_chunk(source_cell)[:, None], (1, 1, 2))
    waves = by_chunk(source_wave).transpose(0, 2, 1).reshape(CHUNKS, 1, 2 * m)
    receivers = by_chunk(receiver_cell)

    steps = CHUNKS + stages - 1
    vmem = pl.BlockSpec(memory_space=pltpu.VMEM)
    smem = pl.BlockSpec(memory_space=pltpu.SMEM)
    stage = lambda t: pl.pallas_call(
        functools.partial(stage_kernel, t, CHUNKS, stages),
        out_shape=(
            pltpu.VMEM((2, m, width), F32),
            pltpu.VMEM(factor.shape, BF16),
            pltpu.VMEM((CHUNKS, 2, m, 128), BF16),
        )
        + ((pltpu.VMEM((2, m, width + 128), BF16),) if t < steps - 1 else ()),
        in_specs=[smem] + [vmem] * 7,
        out_specs=(vmem,) * (4 if t < steps - 1 else 3),
        input_output_aliases={6: 1, 7: 2},
        scratch_shapes=[pltpu.VMEM((1, 2 * m, width), BF16)],
        cost_estimate=pl.CostEstimate(
            flops=int(2 * 2 * 2 * m * 2 * width * width * 0.625),
            bytes_accessed=4 * width * (width + GROUP),
            transcendentals=0,
        ),
        compiler_params=pltpu.CompilerParams(vmem_limit_bytes=LIMIT),
        name="stage",
    )
    post = lambda t: pl.pallas_call(
        functools.partial(post_kernel, t, CHUNKS),
        out_shape=(
            jax.ShapeDtypeStruct((sources, 2, width), F32),
            pltpu.VMEM((8, width), F32),
        ),
        in_specs=[smem, vmem, vmem] + ([pl.BlockSpec(memory_space=pl.ANY), vmem] if t else []),
        out_specs=(pl.BlockSpec(memory_space=pl.ANY), vmem),
        scratch_shapes=[pltpu.VMEM((m, 2, width), F32), pltpu.SemaphoreType.DMA(())],
        input_output_aliases={3: 0, 4: 1} if t else {},
        compiler_params=pltpu.CompilerParams(vmem_limit_bytes=LIMIT),
        cost_estimate=pl.CostEstimate(flops=8 * m * width, bytes_accessed=24 * m * width, transcendentals=0),
        name="post",
    )
    picked = jnp.zeros((CHUNKS, 2, m, receivers.shape[2]), BF16)
    done = ()
    x = jnp.zeros((2, m, width + 128), BF16)
    for t in range(steps):
        field, factor, picked, *y = stage(t)(
            where, x, inflow[min(t, CHUNKS - 1)], cells, waves, receivers, factor, picked
        )
        pairs = [(i, i + 1) for i in range(stages - 1) if 0 <= t - i < CHUNKS]
        if pairs:
            x = lax.ppermute(y[0], "fac", pairs)
        done = post(t)(where, field, adjoint, *done)
        x, done = lax.optimization_barrier((x, done))
    wavefield, grad = done

    rounds = fan_out(stages)
    first = [lax.ppermute(picked, "fac", pairs) for pairs in rounds[0]]
    shards = lax.axis_size(SRC)
    scale = 1.0 / math.sqrt(sources * shards)
    terms = (jnp.sum(grad, axis=0) * scale).reshape(shards, rows)
    terms = lax.all_to_all(terms, SRC, 0, 0, tiled=True)
    first, terms = lax.optimization_barrier((first, terms))
    gradient = jnp.sum(terms, axis=0)[None]
    picked = functools.reduce(jnp.add, first, picked)
    for pairs in rounds[1:]:
        picked = functools.reduce(jnp.add, [lax.ppermute(picked, "fac", p) for p in pairs], picked)
    residual = (picked.astype(F32) - observed).transpose(0, 2, 1, 3).reshape(sources, 2, -1)
    return wavefield[:, None], residual, gradient


def solution(mesh):
    grid = Mesh(mesh.devices.reshape(2, 4, 4, 2, -1), SRC + ("fac",))
    placed = (
        P("fac", SRC, None, None),
        P("fac", SRC, None, None),
        P(SRC),
        P(SRC, None),
        P(SRC, None, None),
        P(SRC, None),
        P(SRC, None, None),
        P(SRC, "fac", None, None),
    )
    return jax.shard_map(
        per_device,
        mesh=grid,
        in_specs=placed,
        out_specs=(P(SRC, "fac", None, None), P(SRC, None, None), P("fac", SRC)),
        check_vma=False,
    )
```

```python
import functools
import math

import jax
import jax.numpy as jnp
from jax import lax
from jax.experimental import pallas as pl
from jax.experimental.pallas import tpu as pltpu
from jax.sharding import Mesh, PartitionSpec as P

SRC = ("zh", "y", "x", "c")
CHUNK = 48
GROUP = 128
LIMIT = 16 << 20
SPLIT = 4
F32, BF16 = jnp.float32, jnp.bfloat16
NT = (((1,), (1,)), ((), ()))
NN = (((1,), (0,)), ((), ()))


def multiply(block, columns, dims):
    return lax.dot_general(block, columns, dims, preferred_element_type=F32)


def group_block(w_ref, group, part, low, high):
    tiles = [w_ref[c, group // 4, 4 * (group % 4) + x, part, :, low:high] for x in range(4) for c in range(2)]
    return jnp.concatenate(tiles, axis=0)


def first_row(chunk, m, sources):
    return pl.multiple_of(jnp.minimum(chunk * m, sources - m), 16)


def stage_kernel(
    step, chunks, stages, sc_ref, x_ref, inflow_ref, cells_ref, wave_ref, receivers_ref, w_ref, _p,
    field_ref, _w, picked_ref, *rest
):
    v_ref = rest[-1]
    last = step == chunks + stages - 2
    owner = sc_ref[0]
    chunk = step - owner
    m, width = inflow_ref.shape[1], inflow_ref.shape[2]
    groups = width // GROUP

    @pl.when((chunk >= 0) & (chunk < chunks))
    def _():
        held = pl.ds(first_row(chunk, m, receivers_ref.shape[0]), m)

        @pl.when(owner == 0)
        def _():
            v_ref[...] = inflow_ref[...].reshape(1, 2 * m, width)
            picked_ref[:, held] = jnp.zeros((2, m, 128), BF16)

        @pl.when(owner != 0)
        def _():
            v_ref[...] = x_ref[:, :, :width].reshape(1, 2 * m, width)
            picked_ref[:, held] = x_ref[:, :, width:]

        straight = v_ref[0]
        crossed = jnp.concatenate([-straight[m:], straight[:m]], axis=0)
        cells = cells_ref[chunk] - owner * width
        waves = wave_ref[chunk]
        rows = lax.broadcasted_iota(jnp.int32, (GROUP, 2 * m), 0)
        reduced, turned = [], []
        for g in range(groups):
            low = GROUP * g
            acc = multiply(group_block(w_ref, g, 0, low + GROUP, width + GROUP), straight[:, low:], NT)
            acc += multiply(group_block(w_ref, g, 1, low + GROUP, width + GROUP), crossed[:, low:], NT)
            value = jnp.where(rows + low == cells, waves, 0.0) - acc
            reduced.append(value.astype(BF16))
            turned.append(jnp.concatenate([-value[:, m:], value[:, :m]], axis=1).astype(BF16))
        reduced, turned = jnp.concatenate(reduced, axis=0), jnp.concatenate(turned, axis=0)
        for g in range(groups):
            low, high = GROUP * g, GROUP * (g + 1)
            acc = multiply(group_block(w_ref, g, 0, 0, high), reduced[:high], NN)
            acc += multiply(group_block(w_ref, g, 1, 0, high), turned[:high], NN)
            acc = acc.T.reshape(2, m, GROUP)
            field_ref[:, :, low:high] = acc
            if not last:
                rest[0][:, :, low:high] = acc.astype(BF16)
        local = receivers_ref[held, :] - owner * width
        tile, lane = local >> 7, local & 127
        for p in range(2):
            got = jnp.zeros((m, 128), F32)
            for t in range(width // 128):
                part = field_ref[p, :, 128 * t : 128 * (t + 1)]
                part = jnp.take_along_axis(part, lane, axis=1, mode="promise_in_bounds")
                got = jnp.where(tile == t, part, got)
            total = picked_ref[p, held] + got.astype(BF16)
            picked_ref[p, held] = total
            if not last:
                rest[0][p, :, width:] = total

    if last:
        @pl.when(owner != stages - 1)
        def _():
            picked_ref[...] = jnp.zeros_like(picked_ref)


def post_kernel(step, chunks, sc_ref, field_ref, adjoint_ref, *refs):
    wave_out, grad_out, rows_ref, sem = refs[-4:]
    owner = sc_ref[0]
    chunk = step - owner
    m, width = field_ref.shape[1], field_ref.shape[2]

    if step == 0:
        grad_out[...] = jnp.zeros_like(grad_out)

    @pl.when((chunk >= 0) & (chunk < chunks))
    def _():
        start = first_row(chunk, m, wave_out.shape[0])
        field = field_ref[...]
        for p in range(2):
            rows_ref[:, p, :] = field[p]
        store = pltpu.make_async_copy(rows_ref, wave_out.at[pl.ds(start, m)], sem)
        store.start()
        prod = field * adjoint_ref[:, pl.ds(start, m), :].astype(F32)
        fresh = lax.broadcasted_iota(jnp.int32, prod.shape, 1) >= chunk * m - start
        prod = jnp.where(fresh, prod, 0.0)
        grad_out[...] += jnp.sum(prod.reshape(2 * m // 8, 8, width), axis=0)
        store.wait()


def place_kernel(sc_ref, own_ref, own_other_ref, far_ref, far_other_ref, out_ref, sems):
    half, core = sc_ref[1], sc_ref[2]
    pieces = (
        (own_ref, core, half),
        (own_other_ref, 1 - core, half),
        (far_ref, core, 1 - half),
        (far_other_ref, 1 - core, 1 - half),
    )
    part = own_ref.shape[0] // SPLIT
    copies = [
        pltpu.make_async_copy(
            ref.at[pl.ds(part * k, part)], out_ref.at[c, h, pl.ds(part * k, part)], sems.at[i, k]
        )
        for i, (ref, c, h) in enumerate(pieces)
        for k in range(SPLIT)
    ]
    for copy in copies:
        copy.start()
    for copy in copies:
        copy.wait()


def swap(array, axis):
    return lax.ppermute(array, axis, [(0, 1), (1, 0)])


def plane_gather(piece):
    plane = lax.axis_size(("y", "x"))
    spread = jnp.broadcast_to(piece[None], (plane,) + piece.shape)
    return lax.all_to_all(spread, ("y", "x"), 0, 0, tiled=True)


def gather_factor(packed, where, others):
    far = swap(packed, "zh")
    own = plane_gather(packed)
    own_other = swap(own, "c")
    far = plane_gather(far)
    far, others = lax.optimization_barrier((far, others))
    far_other = swap(far, "c")
    anywhere = pl.BlockSpec(memory_space=pl.ANY)
    return pl.pallas_call(
        place_kernel,
        out_shape=pltpu.VMEM((2, 2) + own.shape, own.dtype),
        in_specs=[pl.BlockSpec(memory_space=pltpu.SMEM)] + [anywhere] * 4,
        out_specs=pl.BlockSpec(memory_space=pltpu.VMEM),
        scratch_shapes=[pltpu.SemaphoreType.DMA((4, SPLIT))],
        compiler_params=pltpu.CompilerParams(vmem_limit_bytes=LIMIT),
        name="place",
    )(where, own, own_other, far, far_other), *others


def fan_out(stages):
    last = stages - 1
    if stages != 8:
        return [[[(last, i)] for i in range(last)]]
    return [[[(7, 1)], [(7, 4)], [(7, 5)], [(7, 6)]], [[(1, 0), (4, 3), (5, 2)]]]


def per_device(lower, coupling, source_cell, source_wave, inflow, receiver_cell, observed, adjoint):
    owner = lax.axis_index("fac")
    stages = lax.axis_size("fac")
    src = lax.axis_index(SRC)
    width = lower.shape[3]
    rows = lower.shape[1]
    sources = source_cell.shape[0]
    m = min(CHUNK, sources)
    chunks = -(-sources // m)

    split = (src // (GROUP // rows) + 1) * GROUP
    low = jnp.pad(lower[0].transpose(1, 0, 2), ((0, 0), (0, 0), (0, GROUP)))
    high = jnp.pad(coupling[0].transpose(1, 0, 2), ((0, 0), (0, 0), (GROUP, 0)))
    packed = jnp.where(lax.broadcasted_iota(jnp.int32, low.shape, 2) < split, low, high)
    where = jnp.stack([owner, lax.axis_index("zh"), lax.axis_index("c")])

    starts = [min(m * i, sources - m) for i in range(chunks)]
    inflow = inflow.transpose(1, 0, 2)
    adjoint = adjoint[:, 0].transpose(1, 0, 2)
    cells = jnp.stack([jnp.tile(source_cell[i : i + m], 2)[None] for i in starts])
    waves = jnp.stack([source_wave[i : i + m].T.reshape(1, 2 * m) for i in starts])
    factor, inflow, adjoint, cells, waves = gather_factor(packed, where, (inflow, adjoint, cells, waves))

    steps = chunks + stages - 1
    vmem = pl.BlockSpec(memory_space=pltpu.VMEM)
    smem = pl.BlockSpec(memory_space=pltpu.SMEM)
    stage = lambda t: pl.pallas_call(
        functools.partial(stage_kernel, t, chunks, stages),
        out_shape=(
            pltpu.VMEM((2, m, width), F32),
            pltpu.VMEM(factor.shape, BF16),
            pltpu.VMEM((2,) + receiver_cell.shape, BF16),
        )
        + ((pltpu.VMEM((2, m, width + 128), BF16),) if t < steps - 1 else ()),
        in_specs=[smem] + [vmem] * 7,
        out_specs=(vmem,) * (4 if t < steps - 1 else 3),
        input_output_aliases={6: 1, 7: 2},
        scratch_shapes=[pltpu.VMEM((1, 2 * m, width), BF16)],
        cost_estimate=pl.CostEstimate(
            flops=int(2 * 2 * 2 * m * 2 * width * width * 0.625),
            bytes_accessed=4 * width * (width + GROUP),
            transcendentals=0,
        ),
        compiler_params=pltpu.CompilerParams(vmem_limit_bytes=LIMIT),
        name="stage",
    )
    post = lambda t: pl.pallas_call(
        functools.partial(post_kernel, t, chunks),
        out_shape=(
            jax.ShapeDtypeStruct((sources, 2, width), F32),
            pltpu.VMEM((8, width), F32),
        ),
        in_specs=[smem, vmem, vmem] + ([pl.BlockSpec(memory_space=pl.ANY), vmem] if t else []),
        out_specs=(pl.BlockSpec(memory_space=pl.ANY), vmem),
        scratch_shapes=[pltpu.VMEM((m, 2, width), F32), pltpu.SemaphoreType.DMA(())],
        input_output_aliases={3: 0, 4: 1} if t else {},
        compiler_params=pltpu.CompilerParams(vmem_limit_bytes=LIMIT),
        cost_estimate=pl.CostEstimate(flops=8 * m * width, bytes_accessed=24 * m * width, transcendentals=0),
        name="post",
    )
    picked = jnp.zeros((2,) + receiver_cell.shape, BF16)
    done = ()
    x = jnp.zeros((2, m, width + 128), BF16)
    for t in range(steps):
        at = min(t, chunks - 1)
        field, factor, picked, *y = stage(t)(
            where, x, inflow[:, starts[at] : starts[at] + m], cells, waves, receiver_cell, factor, picked
        )
        pairs = [(i, i + 1) for i in range(stages - 1) if 0 <= t - i < chunks]
        if pairs:
            x = lax.ppermute(y[0], "fac", pairs)
        done = post(t)(where, field, adjoint, *done)
        x, done = lax.optimization_barrier((x, done))
    wavefield, grad = done

    rounds = fan_out(stages)
    first = [lax.ppermute(picked, "fac", pairs) for pairs in rounds[0]]
    shards = lax.axis_size(SRC)
    scale = 1.0 / math.sqrt(sources * shards)
    terms = (jnp.sum(grad, axis=0) * scale).reshape(shards, rows)
    terms = lax.all_to_all(terms, SRC, 0, 0, tiled=True)
    first, terms = lax.optimization_barrier((first, terms))
    gradient = jnp.sum(terms, axis=0)[None]
    picked = functools.reduce(jnp.add, first, picked)
    for pairs in rounds[1:]:
        picked = functools.reduce(jnp.add, [lax.ppermute(picked, "fac", p) for p in pairs], picked)
    residual = picked.transpose(1, 0, 2).astype(F32) - observed
    return wavefield[:, None], residual, gradient


def solution(mesh):
    grid = Mesh(mesh.devices.reshape(2, 4, 4, 2, -1), SRC + ("fac",))
    placed = (
        P("fac", SRC, None, None),
        P("fac", SRC, None, None),
        P(SRC),
        P(SRC, None),
        P(SRC, None, None),
        P(SRC, None),
        P(SRC, None, None),
        P(SRC, "fac", None, None),
    )
    return jax.shard_map(
        per_device,
        mesh=grid,
        in_specs=placed,
        out_specs=(P(SRC, "fac", None, None), P(SRC, None, None), P("fac", SRC)),
        check_vma=False,
    )
```

```python
import functools
import math

import jax
import jax.numpy as jnp
from jax import lax
from jax.experimental import pallas as pl
from jax.experimental.pallas import tpu as pltpu
from jax.sharding import Mesh, PartitionSpec as P

SRC = ("zh", "y", "x", "c")
CHUNK = 64
GROUP = 128
LIMIT = 16 << 20
SPLIT = 4
F32, BF16 = jnp.float32, jnp.bfloat16
NT = (((1,), (1,)), ((), ()))
NN = (((1,), (0,)), ((), ()))


def multiply(block, columns, dims):
    return lax.dot_general(block, columns, dims, preferred_element_type=F32)


def group_block(w_ref, group, part, low, high):
    tiles = [w_ref[c, group // 4, 4 * (group % 4) + x, part, :, low:high] for x in range(4) for c in range(2)]
    return jnp.concatenate(tiles, axis=0)


def first_row(chunk, m, sources):
    return pl.multiple_of(jnp.minimum(chunk * m, sources - m), 16)


def stage_kernel(
    step, chunks, stages, sc_ref, x_ref, inflow_ref, cells_ref, wave_ref, receivers_ref, w_ref, _p,
    field_ref, _w, picked_ref, *rest
):
    v_ref = rest[-1]
    last = step == chunks + stages - 2
    owner = sc_ref[0]
    chunk = step - owner
    m, width = inflow_ref.shape[1], inflow_ref.shape[2]
    groups = width // GROUP

    @pl.when((chunk >= 0) & (chunk < chunks))
    def _():
        held = pl.ds(first_row(chunk, m, receivers_ref.shape[0]), m)

        @pl.when(owner == 0)
        def _():
            v_ref[...] = inflow_ref[...].reshape(1, 2 * m, width)
            picked_ref[:, held] = jnp.zeros((2, m, 128), BF16)

        @pl.when(owner != 0)
        def _():
            v_ref[...] = x_ref[:, :, :width].reshape(1, 2 * m, width)
            picked_ref[:, held] = x_ref[:, :, width:]

        straight = v_ref[0]
        crossed = jnp.concatenate([-straight[m:], straight[:m]], axis=0)
        cells = cells_ref[chunk] - owner * width
        waves = wave_ref[chunk]
        rows = lax.broadcasted_iota(jnp.int32, (GROUP, 2 * m), 0)
        reduced, turned = [], []
        for g in range(groups):
            low = GROUP * g
            acc = multiply(group_block(w_ref, g, 0, low + GROUP, width + GROUP), straight[:, low:], NT)
            acc += multiply(group_block(w_ref, g, 1, low + GROUP, width + GROUP), crossed[:, low:], NT)
            value = jnp.where(rows + low == cells, waves, 0.0) - acc
            reduced.append(value.astype(BF16))
            turned.append(jnp.concatenate([-value[:, m:], value[:, :m]], axis=1).astype(BF16))
        reduced, turned = jnp.concatenate(reduced, axis=0), jnp.concatenate(turned, axis=0)
        for g in range(groups):
            low, high = GROUP * g, GROUP * (g + 1)
            acc = multiply(group_block(w_ref, g, 0, 0, high), reduced[:high], NN)
            acc += multiply(group_block(w_ref, g, 1, 0, high), turned[:high], NN)
            acc = acc.T.reshape(2, m, GROUP)
            field_ref[:, :, low:high] = acc
            if not last:
                rest[0][:, :, low:high] = acc.astype(BF16)
        local = receivers_ref[held, :] - owner * width
        tile, lane = local >> 7, local & 127
        for p in range(2):
            got = jnp.zeros((m, 128), F32)
            for t in range(width // 128):
                part = field_ref[p, :, 128 * t : 128 * (t + 1)]
                part = jnp.take_along_axis(part, lane, axis=1, mode="promise_in_bounds")
                got = jnp.where(tile == t, part, got)
            total = picked_ref[p, held] + got.astype(BF16)
            picked_ref[p, held] = total
            if not last:
                rest[0][p, :, width:] = total

    if last:
        @pl.when(owner != stages - 1)
        def _():
            picked_ref[...] = jnp.zeros_like(picked_ref)


def post_kernel(step, chunks, sc_ref, field_ref, adjoint_ref, *refs):
    wave_out, grad_out, rows_ref, sem = refs[-4:]
    owner = sc_ref[0]
    chunk = step - owner
    m, width = field_ref.shape[1], field_ref.shape[2]

    if step == 0:
        grad_out[...] = jnp.zeros_like(grad_out)

    @pl.when((chunk >= 0) & (chunk < chunks))
    def _():
        start = first_row(chunk, m, wave_out.shape[0])
        field = field_ref[...]
        for p in range(2):
            rows_ref[:, p, :] = field[p]
        store = pltpu.make_async_copy(rows_ref, wave_out.at[pl.ds(start, m)], sem)
        store.start()
        prod = field * adjoint_ref[:, pl.ds(start, m), :].astype(F32)
        fresh = lax.broadcasted_iota(jnp.int32, prod.shape, 1) >= chunk * m - start
        prod = jnp.where(fresh, prod, 0.0)
        grad_out[...] += jnp.sum(prod.reshape(2 * m // 8, 8, width), axis=0)
        store.wait()


def place_kernel(sc_ref, own_ref, own_other_ref, far_ref, far_other_ref, out_ref, sems):
    half, core = sc_ref[1], sc_ref[2]
    pieces = (
        (own_ref, core, half),
        (own_other_ref, 1 - core, half),
        (far_ref, core, 1 - half),
        (far_other_ref, 1 - core, 1 - half),
    )
    part = own_ref.shape[0] // SPLIT
    copies = [
        pltpu.make_async_copy(
            ref.at[pl.ds(part * k, part)], out_ref.at[c, h, pl.ds(part * k, part)], sems.at[i, k]
        )
        for i, (ref, c, h) in enumerate(pieces)
        for k in range(SPLIT)
    ]
    for copy in copies:
        copy.start()
    for copy in copies:
        copy.wait()


def swap(array, axis):
    return lax.ppermute(array, axis, [(0, 1), (1, 0)])


def plane_gather(piece):
    plane = lax.axis_size(("y", "x"))
    spread = jnp.broadcast_to(piece[None], (plane,) + piece.shape)
    return lax.all_to_all(spread, ("y", "x"), 0, 0, tiled=True)


def gather_factor(packed, where, others):
    far = swap(packed, "zh")
    own = plane_gather(packed)
    own_other = swap(own, "c")
    far = plane_gather(far)
    far, others = lax.optimization_barrier((far, others))
    far_other = swap(far, "c")
    anywhere = pl.BlockSpec(memory_space=pl.ANY)
    return pl.pallas_call(
        place_kernel,
        out_shape=pltpu.VMEM((2, 2) + own.shape, own.dtype),
        in_specs=[pl.BlockSpec(memory_space=pltpu.SMEM)] + [anywhere] * 4,
        out_specs=pl.BlockSpec(memory_space=pltpu.VMEM),
        scratch_shapes=[pltpu.SemaphoreType.DMA((4, SPLIT))],
        compiler_params=pltpu.CompilerParams(vmem_limit_bytes=LIMIT),
        name="place",
    )(where, own, own_other, far, far_other), *others


def fan_out(stages):
    last = stages - 1
    if stages != 8:
        return [[[(last, i)] for i in range(last)]]
    return [[[(7, 5)], [(7, 2)]], [[(5, 4), (2, 0)]], [[(5, 6), (2, 1), (0, 3)]]]


def per_device(lower, coupling, source_cell, source_wave, inflow, receiver_cell, observed, adjoint):
    owner = lax.axis_index("fac")
    stages = lax.axis_size("fac")
    src = lax.axis_index(SRC)
    width = lower.shape[3]
    rows = lower.shape[1]
    sources = source_cell.shape[0]
    m = min(CHUNK, sources)
    chunks = -(-sources // m)

    split = (src // (GROUP // rows) + 1) * GROUP
    low = jnp.pad(lower[0].transpose(1, 0, 2), ((0, 0), (0, 0), (0, GROUP)))
    high = jnp.pad(coupling[0].transpose(1, 0, 2), ((0, 0), (0, 0), (GROUP, 0)))
    packed = jnp.where(lax.broadcasted_iota(jnp.int32, low.shape, 2) < split, low, high)
    where = jnp.stack([owner, lax.axis_index("zh"), lax.axis_index("c")])

    starts = [min(m * i, sources - m) for i in range(chunks)]
    inflow = inflow.transpose(1, 0, 2)
    adjoint = adjoint[:, 0].transpose(1, 0, 2)
    cells = jnp.stack([jnp.tile(source_cell[i : i + m], 2)[None] for i in starts])
    waves = jnp.stack([source_wave[i : i + m].T.reshape(1, 2 * m) for i in starts])
    factor, inflow, adjoint, cells, waves = gather_factor(packed, where, (inflow, adjoint, cells, waves))

    steps = chunks + stages - 1
    vmem = pl.BlockSpec(memory_space=pltpu.VMEM)
    smem = pl.BlockSpec(memory_space=pltpu.SMEM)
    stage = lambda t: pl.pallas_call(
        functools.partial(stage_kernel, t, chunks, stages),
        out_shape=(
            pltpu.VMEM((2, m, width), F32),
            pltpu.VMEM(factor.shape, BF16),
            pltpu.VMEM((2,) + receiver_cell.shape, BF16),
        )
        + ((pltpu.VMEM((2, m, width + 128), BF16),) if t < steps - 1 else ()),
        in_specs=[smem] + [vmem] * 7,
        out_specs=(vmem,) * (4 if t < steps - 1 else 3),
        input_output_aliases={6: 1, 7: 2},
        scratch_shapes=[pltpu.VMEM((1, 2 * m, width), BF16)],
        cost_estimate=pl.CostEstimate(
            flops=int(2 * 2 * 2 * m * 2 * width * width * 0.625),
            bytes_accessed=4 * width * (width + GROUP),
            transcendentals=0,
        ),
        compiler_params=pltpu.CompilerParams(vmem_limit_bytes=LIMIT),
        name="stage",
    )
    post = lambda t: pl.pallas_call(
        functools.partial(post_kernel, t, chunks),
        out_shape=(
            jax.ShapeDtypeStruct((sources, 2, width), F32),
            pltpu.VMEM((8, width), F32),
        ),
        in_specs=[smem, vmem, vmem] + ([pl.BlockSpec(memory_space=pl.ANY), vmem] if t else []),
        out_specs=(pl.BlockSpec(memory_space=pl.ANY), vmem),
        scratch_shapes=[pltpu.VMEM((m, 2, width), F32), pltpu.SemaphoreType.DMA(())],
        input_output_aliases={3: 0, 4: 1} if t else {},
        compiler_params=pltpu.CompilerParams(vmem_limit_bytes=LIMIT),
        cost_estimate=pl.CostEstimate(flops=8 * m * width, bytes_accessed=24 * m * width, transcendentals=0),
        name="post",
    )
    picked = jnp.zeros((2,) + receiver_cell.shape, BF16)
    done = ()
    x = jnp.zeros((2, m, width + 128), BF16)
    for t in range(steps):
        at = min(t, chunks - 1)
        field, factor, picked, *y = stage(t)(
            where, x, inflow[:, starts[at] : starts[at] + m], cells, waves, receiver_cell, factor, picked
        )
        pairs = [(i, i + 1) for i in range(stages - 1) if 0 <= t - i < chunks]
        if pairs:
            x = lax.ppermute(y[0], "fac", pairs)
        done = post(t)(where, field, adjoint, *done)
        x, done = lax.optimization_barrier((x, done))
    wavefield, grad = done

    rounds = fan_out(stages)
    first = [lax.ppermute(picked, "fac", pairs) for pairs in rounds[0]]
    shards = lax.axis_size(SRC)
    scale = 1.0 / math.sqrt(sources * shards)
    terms = (jnp.sum(grad, axis=0) * scale).reshape(shards, rows)
    terms = lax.all_to_all(terms, SRC, 0, 0, tiled=True)
    first, terms = lax.optimization_barrier((first, terms))
    gradient = jnp.sum(terms, axis=0)[None]
    picked = functools.reduce(jnp.add, first, picked)
    for pairs in rounds[1:]:
        picked = functools.reduce(jnp.add, [lax.ppermute(picked, "fac", p) for p in pairs], picked)
    residual = picked.transpose(1, 0, 2).astype(F32) - observed
    return wavefield[:, None], residual, gradient


def solution(mesh):
    grid = Mesh(mesh.devices.reshape(2, 4, 4, 2, -1), SRC + ("fac",))
    placed = (
        P("fac", SRC, None, None),
        P("fac", SRC, None, None),
        P(SRC),
        P(SRC, None),
        P(SRC, None, None),
        P(SRC, None),
        P(SRC, None, None),
        P(SRC, "fac", None, None),
    )
    return jax.shard_map(
        per_device,
        mesh=grid,
        in_specs=placed,
        out_specs=(P(SRC, "fac", None, None), P(SRC, None, None), P("fac", SRC)),
        check_vma=False,
    )
```

```python
import functools
import math

import jax
import jax.numpy as jnp
from jax import lax
from jax.experimental import pallas as pl
from jax.experimental.pallas import tpu as pltpu
from jax.sharding import Mesh, PartitionSpec as P

SRC = ("zh", "y", "x", "c")
CHUNK = 64
GROUP = 128
LIMIT = 16 << 20
SPLIT = 4
F32, BF16 = jnp.float32, jnp.bfloat16
NT = (((1,), (1,)), ((), ()))
NN = (((1,), (0,)), ((), ()))


def multiply(block, columns, dims):
    return lax.dot_general(block, columns, dims, preferred_element_type=F32)


def group_block(w_ref, group, part, low, high):
    tiles = [w_ref[c, group // 4, 4 * (group % 4) + x, part, :, low:high] for x in range(4) for c in range(2)]
    return jnp.concatenate(tiles, axis=0)


def first_row(chunk, m, sources):
    return pl.multiple_of(jnp.minimum(chunk * m, sources - m), 16)


def stage_kernel(
    step, chunks, stages, sc_ref, x_ref, inflow_ref, cells_ref, wave_ref, receivers_ref, w_ref, _p,
    field_ref, _w, picked_ref, *rest
):
    v_ref = rest[-1]
    last = step == chunks + stages - 2
    owner = sc_ref[0]
    chunk = step - owner
    m, width = inflow_ref.shape[1], inflow_ref.shape[2]
    groups = width // GROUP

    @pl.when((chunk >= 0) & (chunk < chunks))
    def _():
        held = pl.ds(first_row(chunk, m, receivers_ref.shape[0]), m)

        @pl.when(owner == 0)
        def _():
            v_ref[...] = inflow_ref[...].reshape(1, 2 * m, width)
            picked_ref[:, held] = jnp.zeros((2, m, 128), BF16)

        @pl.when(owner != 0)
        def _():
            v_ref[...] = x_ref[:, :, :width].reshape(1, 2 * m, width)
            picked_ref[:, held] = x_ref[:, :, width:]

        straight = v_ref[0]
        crossed = jnp.concatenate([-straight[m:], straight[:m]], axis=0)
        cells = cells_ref[chunk] - owner * width
        waves = wave_ref[chunk]
        rows = lax.broadcasted_iota(jnp.int32, (GROUP, 2 * m), 0)
        reduced, turned = [], []
        for g in range(groups):
            low = GROUP * g
            acc = multiply(group_block(w_ref, g, 0, low + GROUP, width + GROUP), straight[:, low:], NT)
            acc += multiply(group_block(w_ref, g, 1, low + GROUP, width + GROUP), crossed[:, low:], NT)
            value = jnp.where(rows + low == cells, waves, 0.0) - acc
            reduced.append(value.astype(BF16))
            turned.append(jnp.concatenate([-value[:, m:], value[:, :m]], axis=1).astype(BF16))
        reduced, turned = jnp.concatenate(reduced, axis=0), jnp.concatenate(turned, axis=0)
        for g in range(groups):
            low, high = GROUP * g, GROUP * (g + 1)
            acc = multiply(group_block(w_ref, g, 0, 0, high), reduced[:high], NN)
            acc += multiply(group_block(w_ref, g, 1, 0, high), turned[:high], NN)
            acc = acc.T.reshape(2, m, GROUP)
            field_ref[:, :, low:high] = acc
            if not last:
                rest[0][:, :, low:high] = acc.astype(BF16)
        local = receivers_ref[held, :] - owner * width
        tile, lane = local >> 7, local & 127
        for p in range(2):
            got = jnp.zeros((m, 128), F32)
            for t in range(width // 128):
                part = field_ref[p, :, 128 * t : 128 * (t + 1)]
                part = jnp.take_along_axis(part, lane, axis=1, mode="promise_in_bounds")
                got = jnp.where(tile == t, part, got)
            total = picked_ref[p, held] + got.astype(BF16)
            picked_ref[p, held] = total
            if not last:
                rest[0][p, :, width:] = total

    if last:
        @pl.when(owner != stages - 1)
        def _():
            picked_ref[...] = jnp.zeros_like(picked_ref)


def store_rows(field_ref, wave_out, rows_ref, sem, start):
    for p in range(2):
        rows_ref[:, p, :] = field_ref[p]
    store = pltpu.make_async_copy(rows_ref, wave_out.at[pl.ds(start, rows_ref.shape[0])], sem)
    store.start()
    return store


def add_gradient(field_ref, adjoint_ref, grad_out, chunk, start):
    m, width = field_ref.shape[1], field_ref.shape[2]
    prod = field_ref[...] * adjoint_ref[:, pl.ds(start, m), :].astype(F32)
    if adjoint_ref.shape[1] % m:
        fresh = lax.broadcasted_iota(jnp.int32, prod.shape, 1) >= chunk * m - start
        prod = jnp.where(fresh, prod, 0.0)
    grad_out[...] += jnp.sum(prod.reshape(2 * m // 8, 8, width), axis=0)


def post_kernel(step, chunks, sc_ref, field_ref, adjoint_ref, *refs):
    wave_out, grad_out, rows_ref, sem = refs[-4:]
    chunk = step - sc_ref[0]

    if step == 0:
        grad_out[...] = jnp.zeros_like(grad_out)

    @pl.when((chunk >= 0) & (chunk < chunks))
    def _():
        start = first_row(chunk, field_ref.shape[1], wave_out.shape[0])
        store = store_rows(field_ref, wave_out, rows_ref, sem, start)
        add_gradient(field_ref, adjoint_ref, grad_out, chunk, start)
        store.wait()


def last_gradient_kernel(step, chunks, sc_ref, field_ref, adjoint_ref, _g, grad_out):
    chunk = step - sc_ref[0]

    @pl.when((chunk >= 0) & (chunk < chunks))
    def _():
        start = first_row(chunk, field_ref.shape[1], adjoint_ref.shape[1])
        add_gradient(field_ref, adjoint_ref, grad_out, chunk, start)


def last_store_kernel(step, chunks, sc_ref, field_ref, _w, wave_out, rows_ref, sem):
    chunk = step - sc_ref[0]

    @pl.when((chunk >= 0) & (chunk < chunks))
    def _():
        start = first_row(chunk, field_ref.shape[1], wave_out.shape[0])
        store_rows(field_ref, wave_out, rows_ref, sem, start).wait()


def place_kernel(sc_ref, own_ref, own_other_ref, far_ref, far_other_ref, out_ref, sems):
    half, core = sc_ref[1], sc_ref[2]
    pieces = (
        (own_ref, core, half),
        (own_other_ref, 1 - core, half),
        (far_ref, core, 1 - half),
        (far_other_ref, 1 - core, 1 - half),
    )
    part = own_ref.shape[0] // SPLIT
    copies = [
        pltpu.make_async_copy(
            ref.at[pl.ds(part * k, part)], out_ref.at[c, h, pl.ds(part * k, part)], sems.at[i, k]
        )
        for i, (ref, c, h) in enumerate(pieces)
        for k in range(SPLIT)
    ]
    for copy in copies:
        copy.start()
    for copy in copies:
        copy.wait()


def swap(array, axis):
    return lax.ppermute(array, axis, [(0, 1), (1, 0)])


def plane_gather(piece):
    plane = lax.axis_size(("y", "x"))
    spread = jnp.broadcast_to(piece[None], (plane,) + piece.shape)
    return lax.all_to_all(spread, ("y", "x"), 0, 0, tiled=True)


def gather_factor(packed, where, others):
    far = swap(packed, "zh")
    own = plane_gather(packed)
    own_other = swap(own, "c")
    far = plane_gather(far)
    far, others = lax.optimization_barrier((far, others))
    far_other = swap(far, "c")
    anywhere = pl.BlockSpec(memory_space=pl.ANY)
    return pl.pallas_call(
        place_kernel,
        out_shape=pltpu.VMEM((2, 2) + own.shape, own.dtype),
        in_specs=[pl.BlockSpec(memory_space=pltpu.SMEM)] + [anywhere] * 4,
        out_specs=pl.BlockSpec(memory_space=pltpu.VMEM),
        scratch_shapes=[pltpu.SemaphoreType.DMA((4, SPLIT))],
        compiler_params=pltpu.CompilerParams(vmem_limit_bytes=LIMIT),
        name="place",
    )(where, own, own_other, far, far_other), *others


def fan_out(stages):
    last = stages - 1
    if stages != 8:
        return [[[(last, i)] for i in range(last)]]
    return [[[(7, 5)], [(7, 2)]], [[(5, 4), (2, 0)]], [[(5, 6), (2, 1), (0, 3)]]]


def per_device(lower, coupling, source_cell, source_wave, inflow, receiver_cell, observed, adjoint):
    owner = lax.axis_index("fac")
    stages = lax.axis_size("fac")
    src = lax.axis_index(SRC)
    width = lower.shape[3]
    rows = lower.shape[1]
    sources = source_cell.shape[0]
    m = min(CHUNK, sources)
    chunks = -(-sources // m)

    split = (src // (GROUP // rows) + 1) * GROUP
    low = jnp.pad(lower[0].transpose(1, 0, 2), ((0, 0), (0, 0), (0, GROUP)))
    high = jnp.pad(coupling[0].transpose(1, 0, 2), ((0, 0), (0, 0), (GROUP, 0)))
    packed = jnp.where(lax.broadcasted_iota(jnp.int32, low.shape, 2) < split, low, high)
    where = jnp.stack([owner, lax.axis_index("zh"), lax.axis_index("c")])

    starts = [min(m * i, sources - m) for i in range(chunks)]
    inflow = inflow.transpose(1, 0, 2)
    adjoint = adjoint[:, 0].transpose(1, 0, 2)
    cells = jnp.stack([jnp.tile(source_cell[i : i + m], 2)[None] for i in starts])
    waves = jnp.stack([source_wave[i : i + m].T.reshape(1, 2 * m) for i in starts])
    factor, inflow, adjoint, cells, waves = gather_factor(packed, where, (inflow, adjoint, cells, waves))

    steps = chunks + stages - 1
    vmem = pl.BlockSpec(memory_space=pltpu.VMEM)
    smem = pl.BlockSpec(memory_space=pltpu.SMEM)
    stage = lambda t: pl.pallas_call(
        functools.partial(stage_kernel, t, chunks, stages),
        out_shape=(
            pltpu.VMEM((2, m, width), F32),
            pltpu.VMEM(factor.shape, BF16),
            pltpu.VMEM((2,) + receiver_cell.shape, BF16),
        )
        + ((pltpu.VMEM((2, m, width + 128), BF16),) if t < steps - 1 else ()),
        in_specs=[smem] + [vmem] * 7,
        out_specs=(vmem,) * (4 if t < steps - 1 else 3),
        input_output_aliases={6: 1, 7: 2},
        scratch_shapes=[pltpu.VMEM((1, 2 * m, width), BF16)],
        cost_estimate=pl.CostEstimate(
            flops=int(2 * 2 * 2 * m * 2 * width * width * 0.625),
            bytes_accessed=4 * width * (width + GROUP),
            transcendentals=0,
        ),
        compiler_params=pltpu.CompilerParams(vmem_limit_bytes=LIMIT),
        name="stage",
    )
    post = lambda t: pl.pallas_call(
        functools.partial(post_kernel, t, chunks),
        out_shape=(
            jax.ShapeDtypeStruct((sources, 2, width), F32),
            pltpu.VMEM((8, width), F32),
        ),
        in_specs=[smem, vmem, vmem] + ([pl.BlockSpec(memory_space=pl.ANY), vmem] if t else []),
        out_specs=(pl.BlockSpec(memory_space=pl.ANY), vmem),
        scratch_shapes=[pltpu.VMEM((m, 2, width), F32), pltpu.SemaphoreType.DMA(())],
        input_output_aliases={3: 0, 4: 1} if t else {},
        compiler_params=pltpu.CompilerParams(vmem_limit_bytes=LIMIT),
        cost_estimate=pl.CostEstimate(flops=8 * m * width, bytes_accessed=24 * m * width, transcendentals=0),
        name="post",
    )
    last_gradient = pl.pallas_call(
        functools.partial(last_gradient_kernel, steps - 1, chunks),
        out_shape=pltpu.VMEM((8, width), F32),
        in_specs=[smem] + [vmem] * 3,
        out_specs=vmem,
        input_output_aliases={3: 0},
        compiler_params=pltpu.CompilerParams(vmem_limit_bytes=LIMIT),
        cost_estimate=pl.CostEstimate(flops=8 * m * width, bytes_accessed=12 * m * width, transcendentals=0),
        name="last_gradient",
    )
    last_store = pl.pallas_call(
        functools.partial(last_store_kernel, steps - 1, chunks),
        out_shape=jax.ShapeDtypeStruct((sources, 2, width), F32),
        in_specs=[smem, vmem, pl.BlockSpec(memory_space=pl.ANY)],
        out_specs=pl.BlockSpec(memory_space=pl.ANY),
        scratch_shapes=[pltpu.VMEM((m, 2, width), F32), pltpu.SemaphoreType.DMA(())],
        input_output_aliases={2: 0},
        compiler_params=pltpu.CompilerParams(vmem_limit_bytes=LIMIT),
        cost_estimate=pl.CostEstimate(flops=0, bytes_accessed=16 * m * width, transcendentals=0),
        name="last_store",
    )
    picked = jnp.zeros((2,) + receiver_cell.shape, BF16)
    done = ()
    x = jnp.zeros((2, m, width + 128), BF16)
    for t in range(steps):
        at = min(t, chunks - 1)
        field, factor, picked, *y = stage(t)(
            where, x, inflow[:, starts[at] : starts[at] + m], cells, waves, receiver_cell, factor, picked
        )
        pairs = [(i, i + 1) for i in range(stages - 1) if 0 <= t - i < chunks]
        if pairs:
            x = lax.ppermute(y[0], "fac", pairs)
        if t < steps - 1:
            done = post(t)(where, field, adjoint, *done)
            x, done = lax.optimization_barrier((x, done))
    wavefield = last_store(where, field, done[0])
    grad = last_gradient(where, field, adjoint, done[1])

    rounds = fan_out(stages)
    first = [lax.ppermute(picked, "fac", pairs) for pairs in rounds[0]]
    shards = lax.axis_size(SRC)
    scale = 1.0 / math.sqrt(sources * shards)
    terms = (jnp.sum(grad, axis=0) * scale).reshape(shards, rows)
    terms = lax.all_to_all(terms, SRC, 0, 0, tiled=True)
    first, terms, wavefield = lax.optimization_barrier((first, terms, wavefield))
    gradient = jnp.sum(terms, axis=0)[None]
    picked = functools.reduce(jnp.add, first, picked)
    for pairs in rounds[1:]:
        picked = functools.reduce(jnp.add, [lax.ppermute(picked, "fac", p) for p in pairs], picked)
    residual = picked.transpose(1, 0, 2).astype(F32) - observed
    return wavefield[:, None], residual, gradient


def solution(mesh):
    grid = Mesh(mesh.devices.reshape(2, 4, 4, 2, -1), SRC + ("fac",))
    placed = (
        P("fac", SRC, None, None),
        P("fac", SRC, None, None),
        P(SRC),
        P(SRC, None),
        P(SRC, None, None),
        P(SRC, None),
        P(SRC, None, None),
        P(SRC, "fac", None, None),
    )
    return jax.shard_map(
        per_device,
        mesh=grid,
        in_specs=placed,
        out_specs=(P(SRC, "fac", None, None), P(SRC, None, None), P("fac", SRC)),
        check_vma=False,
    )
```

```python
import functools
import math

import jax
import jax.numpy as jnp
from jax import lax
from jax.experimental import pallas as pl
from jax.experimental.pallas import tpu as pltpu
from jax.sharding import Mesh, PartitionSpec as P

SRC = ("zh", "y", "x", "c")
CHUNK = 64
GROUP = 128
LIMIT = 16 << 20
SPLIT = 4
F32, BF16 = jnp.float32, jnp.bfloat16
NT = (((1,), (1,)), ((), ()))
NN = (((1,), (0,)), ((), ()))


def multiply(block, columns, dims):
    return lax.dot_general(block, columns, dims, preferred_element_type=F32)


def group_block(w_ref, group, part, low, high):
    tiles = [w_ref[c, group // 4, 4 * (group % 4) + x, part, :, low:high] for x in range(4) for c in range(2)]
    return jnp.concatenate(tiles, axis=0)


def first_row(chunk, m, sources):
    return pl.multiple_of(jnp.minimum(chunk * m, sources - m), 16)


def stage_kernel(
    step, chunks, stages, sc_ref, x_ref, inflow_ref, cells_ref, wave_ref, receivers_ref, w_ref, _p,
    field_ref, _w, picked_ref, *rest
):
    v_ref = rest[-1]
    last = step == chunks + stages - 2
    owner = sc_ref[0]
    chunk = step - owner
    m, width = inflow_ref.shape[1], inflow_ref.shape[2]
    groups = width // GROUP

    @pl.when((chunk >= 0) & (chunk < chunks))
    def _():
        held = pl.ds(first_row(chunk, m, receivers_ref.shape[0]), m)

        @pl.when(owner == 0)
        def _():
            v_ref[...] = inflow_ref[...].reshape(1, 2 * m, width)
            picked_ref[:, held] = jnp.zeros((2, m, 128), BF16)

        @pl.when(owner != 0)
        def _():
            v_ref[...] = x_ref[:, :, :width].reshape(1, 2 * m, width)
            picked_ref[:, held] = x_ref[:, :, width:]

        straight = v_ref[0]
        crossed = jnp.concatenate([-straight[m:], straight[:m]], axis=0)
        cells = cells_ref[chunk] - owner * width
        waves = wave_ref[chunk]
        rows = lax.broadcasted_iota(jnp.int32, (GROUP, 2 * m), 0)
        reduced, turned = [], []
        for g in range(groups):
            low = GROUP * g
            acc = multiply(group_block(w_ref, g, 0, low + GROUP, width + GROUP), straight[:, low:], NT)
            acc += multiply(group_block(w_ref, g, 1, low + GROUP, width + GROUP), crossed[:, low:], NT)
            value = jnp.where(rows + low == cells, waves, 0.0) - acc
            reduced.append(value.astype(BF16))
            turned.append(jnp.concatenate([-value[:, m:], value[:, :m]], axis=1).astype(BF16))
        reduced, turned = jnp.concatenate(reduced, axis=0), jnp.concatenate(turned, axis=0)
        for g in range(groups):
            low, high = GROUP * g, GROUP * (g + 1)
            acc = multiply(group_block(w_ref, g, 0, 0, high), reduced[:high], NN)
            acc += multiply(group_block(w_ref, g, 1, 0, high), turned[:high], NN)
            acc = acc.T.reshape(2, m, GROUP)
            field_ref[:, :, low:high] = acc
            if not last:
                rest[0][:, :, low:high] = acc.astype(BF16)
        local = receivers_ref[held, :] - owner * width
        tile, lane = local >> 7, local & 127
        for p in range(2):
            got = jnp.zeros((m, 128), F32)
            for t in range(width // 128):
                part = field_ref[p, :, 128 * t : 128 * (t + 1)]
                part = jnp.take_along_axis(part, lane, axis=1, mode="promise_in_bounds")
                got = jnp.where(tile == t, part, got)
            total = picked_ref[p, held] + got.astype(BF16)
            picked_ref[p, held] = total
            if not last:
                rest[0][p, :, width:] = total

    if last:
        @pl.when(owner != stages - 1)
        def _():
            picked_ref[...] = jnp.zeros_like(picked_ref)


def store_rows(field_ref, wave_out, rows_ref, sem, start):
    for p in range(2):
        rows_ref[:, p, :] = field_ref[p]
    store = pltpu.make_async_copy(rows_ref, wave_out.at[pl.ds(start, rows_ref.shape[0])], sem)
    store.start()
    return store


def add_gradient(field_ref, adjoint_ref, grad_out, chunk, start):
    m, width = field_ref.shape[1], field_ref.shape[2]
    prod = field_ref[...] * adjoint_ref[:, pl.ds(start, m), :].astype(F32)
    if adjoint_ref.shape[1] % m:
        fresh = lax.broadcasted_iota(jnp.int32, prod.shape, 1) >= chunk * m - start
        prod = jnp.where(fresh, prod, 0.0)
    grad_out[...] += jnp.sum(prod.reshape(2 * m // 8, 8, width), axis=0)


def post_kernel(step, chunks, sc_ref, field_ref, adjoint_ref, *refs):
    wave_out, grad_out, rows_ref, sem = refs[-4:]
    chunk = step - sc_ref[0]

    if step == 0:
        grad_out[...] = jnp.zeros_like(grad_out)

    @pl.when((chunk >= 0) & (chunk < chunks))
    def _():
        start = first_row(chunk, field_ref.shape[1], wave_out.shape[0])
        store = store_rows(field_ref, wave_out, rows_ref, sem, start)
        add_gradient(field_ref, adjoint_ref, grad_out, chunk, start)
        store.wait()


def last_gradient_kernel(step, chunks, sc_ref, field_ref, adjoint_ref, _g, grad_out):
    chunk = step - sc_ref[0]

    @pl.when((chunk >= 0) & (chunk < chunks))
    def _():
        start = first_row(chunk, field_ref.shape[1], adjoint_ref.shape[1])
        add_gradient(field_ref, adjoint_ref, grad_out, chunk, start)


def last_store_kernel(step, chunks, sc_ref, field_ref, _w, wave_out, rows_ref, sem):
    chunk = step - sc_ref[0]

    @pl.when((chunk >= 0) & (chunk < chunks))
    def _():
        start = first_row(chunk, field_ref.shape[1], wave_out.shape[0])
        store_rows(field_ref, wave_out, rows_ref, sem, start).wait()


def place_kernel(sc_ref, own_ref, own_other_ref, far_ref, far_other_ref, out_ref, sems):
    half, core = sc_ref[1], sc_ref[2]
    pieces = (
        (own_ref, core, half),
        (own_other_ref, 1 - core, half),
        (far_ref, core, 1 - half),
        (far_other_ref, 1 - core, 1 - half),
    )
    part = own_ref.shape[0] // SPLIT
    copies = [
        pltpu.make_async_copy(
            ref.at[pl.ds(part * k, part)], out_ref.at[c, h, pl.ds(part * k, part)], sems.at[i, k]
        )
        for i, (ref, c, h) in enumerate(pieces)
        for k in range(SPLIT)
    ]
    for copy in copies:
        copy.start()
    for copy in copies:
        copy.wait()


def swap(array, axis):
    return lax.ppermute(array, axis, [(0, 1), (1, 0)])


def plane_gather(piece):
    plane = lax.axis_size(("y", "x"))
    spread = jnp.broadcast_to(piece[None], (plane,) + piece.shape)
    return lax.all_to_all(spread, ("y", "x"), 0, 0, tiled=True)


def gather_factor(packed, where, others):
    far = swap(packed, "zh")
    own = plane_gather(packed)
    own_other = swap(own, "c")
    far = plane_gather(far)
    far, others = lax.optimization_barrier((far, others))
    far_other = swap(far, "c")
    anywhere = pl.BlockSpec(memory_space=pl.ANY)
    return pl.pallas_call(
        place_kernel,
        out_shape=pltpu.VMEM((2, 2) + own.shape, own.dtype),
        in_specs=[pl.BlockSpec(memory_space=pltpu.SMEM)] + [anywhere] * 4,
        out_specs=pl.BlockSpec(memory_space=pltpu.VMEM),
        scratch_shapes=[pltpu.SemaphoreType.DMA((4, SPLIT))],
        compiler_params=pltpu.CompilerParams(vmem_limit_bytes=LIMIT),
        name="place",
    )(where, own, own_other, far, far_other), *others


def fan_out(stages):
    last = stages - 1
    if stages != 8:
        return [[[(last, i)] for i in range(last)]]
    return [[[(7, 6)], [(7, 4)], [(7, 1)]], [[(4, 5), (1, 0)]], [[(1, 2), (0, 3)]]]


def per_device(lower, coupling, source_cell, source_wave, inflow, receiver_cell, observed, adjoint):
    owner = lax.axis_index("fac")
    stages = lax.axis_size("fac")
    src = lax.axis_index(SRC)
    width = lower.shape[3]
    rows = lower.shape[1]
    sources = source_cell.shape[0]
    m = min(CHUNK, sources)
    chunks = -(-sources // m)

    split = (src // (GROUP // rows) + 1) * GROUP
    low = jnp.pad(lower[0].transpose(1, 0, 2), ((0, 0), (0, 0), (0, GROUP)))
    high = jnp.pad(coupling[0].transpose(1, 0, 2), ((0, 0), (0, 0), (GROUP, 0)))
    packed = jnp.where(lax.broadcasted_iota(jnp.int32, low.shape, 2) < split, low, high)
    where = jnp.stack([owner, lax.axis_index("zh"), lax.axis_index("c")])

    starts = [min(m * i, sources - m) for i in range(chunks)]
    inflow = inflow.transpose(1, 0, 2)
    adjoint = adjoint[:, 0].transpose(1, 0, 2)
    cells = jnp.stack([jnp.tile(source_cell[i : i + m], 2)[None] for i in starts])
    waves = jnp.stack([source_wave[i : i + m].T.reshape(1, 2 * m) for i in starts])
    factor, inflow, adjoint, cells, waves = gather_factor(packed, where, (inflow, adjoint, cells, waves))

    steps = chunks + stages - 1
    vmem = pl.BlockSpec(memory_space=pltpu.VMEM)
    smem = pl.BlockSpec(memory_space=pltpu.SMEM)
    stage = lambda t: pl.pallas_call(
        functools.partial(stage_kernel, t, chunks, stages),
        out_shape=(
            pltpu.VMEM((2, m, width), F32),
            pltpu.VMEM(factor.shape, BF16),
            pltpu.VMEM((2,) + receiver_cell.shape, BF16),
        )
        + ((pltpu.VMEM((2, m, width + 128), BF16),) if t < steps - 1 else ()),
        in_specs=[smem] + [vmem] * 7,
        out_specs=(vmem,) * (4 if t < steps - 1 else 3),
        input_output_aliases={6: 1, 7: 2},
        scratch_shapes=[pltpu.VMEM((1, 2 * m, width), BF16)],
        cost_estimate=pl.CostEstimate(
            flops=int(2 * 2 * 2 * m * 2 * width * width * 0.625),
            bytes_accessed=4 * width * (width + GROUP),
            transcendentals=0,
        ),
        compiler_params=pltpu.CompilerParams(vmem_limit_bytes=LIMIT),
        name="stage",
    )
    post = lambda t: pl.pallas_call(
        functools.partial(post_kernel, t, chunks),
        out_shape=(
            jax.ShapeDtypeStruct((sources, 2, width), F32),
            pltpu.VMEM((8, width), F32),
        ),
        in_specs=[smem, vmem, vmem] + ([pl.BlockSpec(memory_space=pl.ANY), vmem] if t else []),
        out_specs=(pl.BlockSpec(memory_space=pl.ANY), vmem),
        scratch_shapes=[pltpu.VMEM((m, 2, width), F32), pltpu.SemaphoreType.DMA(())],
        input_output_aliases={3: 0, 4: 1} if t else {},
        compiler_params=pltpu.CompilerParams(vmem_limit_bytes=LIMIT),
        cost_estimate=pl.CostEstimate(flops=8 * m * width, bytes_accessed=24 * m * width, transcendentals=0),
        name="post",
    )
    last_gradient = pl.pallas_call(
        functools.partial(last_gradient_kernel, steps - 1, chunks),
        out_shape=pltpu.VMEM((8, width), F32),
        in_specs=[smem] + [vmem] * 3,
        out_specs=vmem,
        input_output_aliases={3: 0},
        compiler_params=pltpu.CompilerParams(vmem_limit_bytes=LIMIT),
        cost_estimate=pl.CostEstimate(flops=8 * m * width, bytes_accessed=12 * m * width, transcendentals=0),
        name="last_gradient",
    )
    last_store = pl.pallas_call(
        functools.partial(last_store_kernel, steps - 1, chunks),
        out_shape=jax.ShapeDtypeStruct((sources, 2, width), F32),
        in_specs=[smem, vmem, pl.BlockSpec(memory_space=pl.ANY)],
        out_specs=pl.BlockSpec(memory_space=pl.ANY),
        scratch_shapes=[pltpu.VMEM((m, 2, width), F32), pltpu.SemaphoreType.DMA(())],
        input_output_aliases={2: 0},
        compiler_params=pltpu.CompilerParams(vmem_limit_bytes=LIMIT),
        cost_estimate=pl.CostEstimate(flops=0, bytes_accessed=16 * m * width, transcendentals=0),
        name="last_store",
    )
    picked = jnp.zeros((2,) + receiver_cell.shape, BF16)
    done = ()
    x = jnp.zeros((2, m, width + 128), BF16)
    for t in range(steps):
        at = min(t, chunks - 1)
        field, factor, picked, *y = stage(t)(
            where, x, inflow[:, starts[at] : starts[at] + m], cells, waves, receiver_cell, factor, picked
        )
        pairs = [(i, i + 1) for i in range(stages - 1) if 0 <= t - i < chunks]
        if pairs:
            x = lax.ppermute(y[0], "fac", pairs)
        if t < steps - 1:
            done = post(t)(where, field, adjoint, *done)
            x, done = lax.optimization_barrier((x, done))
    wavefield = last_store(where, field, done[0])
    grad = last_gradient(where, field, adjoint, done[1])

    rounds = fan_out(stages)
    first = [lax.ppermute(picked, "fac", pairs) for pairs in rounds[0]]
    shards = lax.axis_size(SRC)
    scale = 1.0 / math.sqrt(sources * shards)
    terms = (jnp.sum(grad, axis=0) * scale).reshape(shards, rows)
    terms = lax.all_to_all(terms, SRC, 0, 0, tiled=True)
    first, terms, wavefield = lax.optimization_barrier((first, terms, wavefield))
    gradient = jnp.sum(terms, axis=0)[None]
    picked = functools.reduce(jnp.add, first, picked)
    for pairs in rounds[1:]:
        picked = functools.reduce(jnp.add, [lax.ppermute(picked, "fac", p) for p in pairs], picked)
    residual = picked.transpose(1, 0, 2).astype(F32) - observed
    return wavefield[:, None], residual, gradient


def solution(mesh):
    grid = Mesh(mesh.devices.reshape(2, 4, 4, 2, -1), SRC + ("fac",))
    placed = (
        P("fac", SRC, None, None),
        P("fac", SRC, None, None),
        P(SRC),
        P(SRC, None),
        P(SRC, None, None),
        P(SRC, None),
        P(SRC, None, None),
        P(SRC, "fac", None, None),
    )
    return jax.shard_map(
        per_device,
        mesh=grid,
        in_specs=placed,
        out_specs=(P(SRC, "fac", None, None), P(SRC, None, None), P("fac", SRC)),
        check_vma=False,
    )
```

```python
import functools
import math

import jax
import jax.numpy as jnp
from jax import lax
from jax.experimental import pallas as pl
from jax.experimental.pallas import tpu as pltpu
from jax.sharding import Mesh, PartitionSpec as P

SRC = ("zh", "y", "x", "c")
CHUNK = 64
GROUP = 128
LIMIT = 16 << 20
SPLIT = 4
F32, BF16 = jnp.float32, jnp.bfloat16
NT = (((1,), (1,)), ((), ()))
NN = (((1,), (0,)), ((), ()))


def multiply(block, columns, dims):
    return lax.dot_general(block, columns, dims, preferred_element_type=F32)


def group_block(w_ref, group, part, low, high):
    tiles = [w_ref[c, group // 4, 4 * (group % 4) + x, part, :, low:high] for x in range(4) for c in range(2)]
    return jnp.concatenate(tiles, axis=0)


def first_row(chunk, m, sources):
    return pl.multiple_of(jnp.minimum(chunk * m, sources - m), 16)


def stage_kernel(
    step, chunks, stages, sc_ref, x_ref, inflow_ref, cells_ref, wave_ref, receivers_ref, w_ref, _p,
    field_ref, _w, picked_ref, *rest
):
    v_ref = rest[-1]
    last = step == chunks + stages - 2
    owner = sc_ref[0]
    chunk = step - owner
    m, width = inflow_ref.shape[1], inflow_ref.shape[2]
    groups = width // GROUP

    @pl.when((chunk >= 0) & (chunk < chunks))
    def _():
        held = pl.ds(first_row(chunk, m, receivers_ref.shape[0]), m)

        @pl.when(owner == 0)
        def _():
            v_ref[...] = inflow_ref[...].reshape(1, 2 * m, width)
            picked_ref[:, held] = jnp.zeros((2, m, 128), BF16)

        @pl.when(owner != 0)
        def _():
            v_ref[...] = x_ref[:, :, :width].reshape(1, 2 * m, width)
            picked_ref[:, held] = x_ref[:, :, width:]

        straight = v_ref[0]
        crossed = jnp.concatenate([-straight[m:], straight[:m]], axis=0)
        cells = cells_ref[chunk] - owner * width
        waves = wave_ref[chunk]
        rows = lax.broadcasted_iota(jnp.int32, (GROUP, 2 * m), 0)
        reduced, turned = [], []
        for g in range(groups):
            low = GROUP * g
            acc = multiply(group_block(w_ref, g, 0, low + GROUP, width + GROUP), straight[:, low:], NT)
            acc += multiply(group_block(w_ref, g, 1, low + GROUP, width + GROUP), crossed[:, low:], NT)
            value = jnp.where(rows + low == cells, waves, 0.0) - acc
            reduced.append(value.astype(BF16))
            turned.append(jnp.concatenate([-value[:, m:], value[:, :m]], axis=1).astype(BF16))
        reduced, turned = jnp.concatenate(reduced, axis=0), jnp.concatenate(turned, axis=0)
        for g in range(groups):
            low, high = GROUP * g, GROUP * (g + 1)
            acc = multiply(group_block(w_ref, g, 0, 0, high), reduced[:high], NN)
            acc += multiply(group_block(w_ref, g, 1, 0, high), turned[:high], NN)
            acc = acc.T.reshape(2, m, GROUP)
            field_ref[:, :, low:high] = acc
            if not last:
                rest[0][:, :, low:high] = acc.astype(BF16)
        local = receivers_ref[held, :] - owner * width
        tile, lane = local >> 7, local & 127
        for p in range(2):
            got = jnp.zeros((m, 128), F32)
            for t in range(width // 128):
                part = field_ref[p, :, 128 * t : 128 * (t + 1)]
                part = jnp.take_along_axis(part, lane, axis=1, mode="promise_in_bounds")
                got = jnp.where(tile == t, part, got)
            total = picked_ref[p, held] + got.astype(BF16)
            picked_ref[p, held] = total
            if not last:
                rest[0][p, :, width:] = total

    if last:
        @pl.when(owner != stages - 1)
        def _():
            picked_ref[...] = jnp.zeros_like(picked_ref)


def store_rows(field_ref, wave_out, rows_ref, sem, start):
    for p in range(2):
        rows_ref[:, p, :] = field_ref[p]
    store = pltpu.make_async_copy(rows_ref, wave_out.at[pl.ds(start, rows_ref.shape[0])], sem)
    store.start()
    return store


def add_gradient(field_ref, adjoint_ref, grad_out, chunk, start):
    m, width = field_ref.shape[1], field_ref.shape[2]
    prod = field_ref[...] * adjoint_ref[:, pl.ds(start, m), :].astype(F32)
    if adjoint_ref.shape[1] % m:
        fresh = lax.broadcasted_iota(jnp.int32, prod.shape, 1) >= chunk * m - start
        prod = jnp.where(fresh, prod, 0.0)
    grad_out[...] += jnp.sum(prod.reshape(2 * m // 8, 8, width), axis=0)


def post_kernel(step, chunks, sc_ref, field_ref, adjoint_ref, *refs):
    wave_out, grad_out, rows_ref, sem = refs[-4:]
    chunk = step - sc_ref[0]

    if step == 0:
        grad_out[...] = jnp.zeros_like(grad_out)

    @pl.when((chunk >= 0) & (chunk < chunks))
    def _():
        start = first_row(chunk, field_ref.shape[1], wave_out.shape[0])
        store = store_rows(field_ref, wave_out, rows_ref, sem, start)
        add_gradient(field_ref, adjoint_ref, grad_out, chunk, start)
        store.wait()


def last_gradient_kernel(step, chunks, sc_ref, field_ref, adjoint_ref, _g, grad_out):
    chunk = step - sc_ref[0]

    @pl.when((chunk >= 0) & (chunk < chunks))
    def _():
        start = first_row(chunk, field_ref.shape[1], adjoint_ref.shape[1])
        add_gradient(field_ref, adjoint_ref, grad_out, chunk, start)


def last_store_kernel(step, chunks, sc_ref, field_ref, _w, wave_out, rows_ref, sem):
    chunk = step - sc_ref[0]

    @pl.when((chunk >= 0) & (chunk < chunks))
    def _():
        start = first_row(chunk, field_ref.shape[1], wave_out.shape[0])
        store_rows(field_ref, wave_out, rows_ref, sem, start).wait()


def place_kernel(sc_ref, own_ref, own_other_ref, far_ref, far_other_ref, out_ref, sems):
    half, core = sc_ref[1], sc_ref[2]
    pieces = (
        (own_ref, core, half),
        (own_other_ref, 1 - core, half),
        (far_ref, core, 1 - half),
        (far_other_ref, 1 - core, 1 - half),
    )
    part = own_ref.shape[0] // SPLIT
    copies = [
        pltpu.make_async_copy(
            ref.at[pl.ds(part * k, part)], out_ref.at[c, h, pl.ds(part * k, part)], sems.at[i, k]
        )
        for i, (ref, c, h) in enumerate(pieces)
        for k in range(SPLIT)
    ]
    for copy in copies:
        copy.start()
    for copy in copies:
        copy.wait()


def swap(array, axis):
    return lax.ppermute(array, axis, [(0, 1), (1, 0)])


def plane_gather(piece):
    plane = lax.axis_size(("y", "x"))
    spread = jnp.broadcast_to(piece[None], (plane,) + piece.shape)
    return lax.all_to_all(spread, ("y", "x"), 0, 0, tiled=True)


def gather_factor(packed, where, others):
    far = swap(packed, "zh")
    own = plane_gather(packed)
    own_other = swap(own, "c")
    far = plane_gather(far)
    far, others = lax.optimization_barrier((far, others))
    far_other = swap(far, "c")
    anywhere = pl.BlockSpec(memory_space=pl.ANY)
    return pl.pallas_call(
        place_kernel,
        out_shape=pltpu.VMEM((2, 2) + own.shape, own.dtype),
        in_specs=[pl.BlockSpec(memory_space=pltpu.SMEM)] + [anywhere] * 4,
        out_specs=pl.BlockSpec(memory_space=pltpu.VMEM),
        scratch_shapes=[pltpu.SemaphoreType.DMA((4, SPLIT))],
        compiler_params=pltpu.CompilerParams(vmem_limit_bytes=LIMIT),
        name="place",
    )(where, own, own_other, far, far_other), *others


def fan_out(stages):
    last = stages - 1
    if stages != 8:
        return [[[(last, i)] for i in range(last)]]
    return [[[(7, 6)], [(7, 2)]], [[(2, 0), (6, 5)]], [[(2, 1), (0, 3), (6, 4)]]]


def per_device(lower, coupling, source_cell, source_wave, inflow, receiver_cell, observed, adjoint):
    owner = lax.axis_index("fac")
    stages = lax.axis_size("fac")
    src = lax.axis_index(SRC)
    width = lower.shape[3]
    rows = lower.shape[1]
    sources = source_cell.shape[0]
    m = min(CHUNK, sources)
    chunks = -(-sources // m)

    split = (src // (GROUP // rows) + 1) * GROUP
    low = jnp.pad(lower[0].transpose(1, 0, 2), ((0, 0), (0, 0), (0, GROUP)))
    high = jnp.pad(coupling[0].transpose(1, 0, 2), ((0, 0), (0, 0), (GROUP, 0)))
    packed = jnp.where(lax.broadcasted_iota(jnp.int32, low.shape, 2) < split, low, high)
    where = jnp.stack([owner, lax.axis_index("zh"), lax.axis_index("c")])

    starts = [min(m * i, sources - m) for i in range(chunks)]
    inflow = inflow.transpose(1, 0, 2)
    adjoint = adjoint[:, 0].transpose(1, 0, 2)
    cells = jnp.stack([jnp.tile(source_cell[i : i + m], 2)[None] for i in starts])
    waves = jnp.stack([source_wave[i : i + m].T.reshape(1, 2 * m) for i in starts])
    factor, inflow, adjoint, cells, waves = gather_factor(packed, where, (inflow, adjoint, cells, waves))

    steps = chunks + stages - 1
    vmem = pl.BlockSpec(memory_space=pltpu.VMEM)
    smem = pl.BlockSpec(memory_space=pltpu.SMEM)
    stage = lambda t: pl.pallas_call(
        functools.partial(stage_kernel, t, chunks, stages),
        out_shape=(
            pltpu.VMEM((2, m, width), F32),
            pltpu.VMEM(factor.shape, BF16),
            pltpu.VMEM((2,) + receiver_cell.shape, BF16),
        )
        + ((pltpu.VMEM((2, m, width + 128), BF16),) if t < steps - 1 else ()),
        in_specs=[smem] + [vmem] * 7,
        out_specs=(vmem,) * (4 if t < steps - 1 else 3),
        input_output_aliases={6: 1, 7: 2},
        scratch_shapes=[pltpu.VMEM((1, 2 * m, width), BF16)],
        cost_estimate=pl.CostEstimate(
            flops=int(2 * 2 * 2 * m * 2 * width * width * 0.625),
            bytes_accessed=4 * width * (width + GROUP),
            transcendentals=0,
        ),
        compiler_params=pltpu.CompilerParams(vmem_limit_bytes=LIMIT),
        name="stage",
    )
    post = lambda t: pl.pallas_call(
        functools.partial(post_kernel, t, chunks),
        out_shape=(
            jax.ShapeDtypeStruct((sources, 2, width), F32),
            pltpu.VMEM((8, width), F32),
        ),
        in_specs=[smem, vmem, vmem] + ([pl.BlockSpec(memory_space=pl.ANY), vmem] if t else []),
        out_specs=(pl.BlockSpec(memory_space=pl.ANY), vmem),
        scratch_shapes=[pltpu.VMEM((m, 2, width), F32), pltpu.SemaphoreType.DMA(())],
        input_output_aliases={3: 0, 4: 1} if t else {},
        compiler_params=pltpu.CompilerParams(vmem_limit_bytes=LIMIT),
        cost_estimate=pl.CostEstimate(flops=8 * m * width, bytes_accessed=24 * m * width, transcendentals=0),
        name="post",
    )
    last_gradient = pl.pallas_call(
        functools.partial(last_gradient_kernel, steps - 1, chunks),
        out_shape=pltpu.VMEM((8, width), F32),
        in_specs=[smem] + [vmem] * 3,
        out_specs=vmem,
        input_output_aliases={3: 0},
        compiler_params=pltpu.CompilerParams(vmem_limit_bytes=LIMIT),
        cost_estimate=pl.CostEstimate(flops=8 * m * width, bytes_accessed=12 * m * width, transcendentals=0),
        name="last_gradient",
    )
    last_store = pl.pallas_call(
        functools.partial(last_store_kernel, steps - 1, chunks),
        out_shape=jax.ShapeDtypeStruct((sources, 2, width), F32),
        in_specs=[smem, vmem, pl.BlockSpec(memory_space=pl.ANY)],
        out_specs=pl.BlockSpec(memory_space=pl.ANY),
        scratch_shapes=[pltpu.VMEM((m, 2, width), F32), pltpu.SemaphoreType.DMA(())],
        input_output_aliases={2: 0},
        compiler_params=pltpu.CompilerParams(vmem_limit_bytes=LIMIT),
        cost_estimate=pl.CostEstimate(flops=0, bytes_accessed=16 * m * width, transcendentals=0),
        name="last_store",
    )
    picked = jnp.zeros((2,) + receiver_cell.shape, BF16)
    done = ()
    x = jnp.zeros((2, m, width + 128), BF16)
    for t in range(steps):
        at = min(t, chunks - 1)
        field, factor, picked, *y = stage(t)(
            where, x, inflow[:, starts[at] : starts[at] + m], cells, waves, receiver_cell, factor, picked
        )
        pairs = [(i, i + 1) for i in range(stages - 1) if 0 <= t - i < chunks]
        if pairs:
            x = lax.ppermute(y[0], "fac", pairs)
        if t < steps - 1:
            done = post(t)(where, field, adjoint, *done)
            x, done = lax.optimization_barrier((x, done))
    wavefield = last_store(where, field, done[0])
    grad = last_gradient(where, field, adjoint, done[1])

    rounds = fan_out(stages)
    first = [lax.ppermute(picked, "fac", pairs) for pairs in rounds[0]]
    shards = lax.axis_size(SRC)
    scale = 1.0 / math.sqrt(sources * shards)
    terms = (jnp.sum(grad, axis=0) * scale).reshape(shards, rows)
    terms = lax.all_to_all(terms, SRC, 0, 0, tiled=True)
    first, terms, wavefield = lax.optimization_barrier((first, terms, wavefield))
    gradient = jnp.sum(terms, axis=0)[None]
    picked = functools.reduce(jnp.add, first, picked)
    for pairs in rounds[1:]:
        picked = functools.reduce(jnp.add, [lax.ppermute(picked, "fac", p) for p in pairs], picked)
    residual = picked.transpose(1, 0, 2).astype(F32) - observed
    return wavefield[:, None], residual, gradient


def solution(mesh):
    grid = Mesh(mesh.devices.reshape(2, 4, 4, 2, -1), SRC + ("fac",))
    placed = (
        P("fac", SRC, None, None),
        P("fac", SRC, None, None),
        P(SRC),
        P(SRC, None),
        P(SRC, None, None),
        P(SRC, None),
        P(SRC, None, None),
        P(SRC, "fac", None, None),
    )
    return jax.shard_map(
        per_device,
        mesh=grid,
        in_specs=placed,
        out_specs=(P(SRC, "fac", None, None), P(SRC, None, None), P("fac", SRC)),
        check_vma=False,
    )
```
